32 devices in a mesh: dp: 8 (over y, x, core), tensor: 4 (over z).
Axes of the slice: x: 2, y: 2, z: 4, core: 2. Of those that a mesh axis runs over, the one named last changes fastest.
Arguments:
- tokens: bfloat16 [16384, 2048], P(('dp', 'tensor')), may hold values from -6 to 6
- w_query: bfloat16 [2048, 2048], P('dp', 'tensor'), may hold values from -0.125 to 0.125
- w_key: bfloat16 [2048, 2048], P('dp', 'tensor'), may hold values from -0.125 to 0.125
- w_value: bfloat16 [2048, 2048], P('dp', 'tensor'), may hold values from -0.125 to 0.125
- w_output: bfloat16 [2048, 2048], P('dp', 'tensor'), may hold values from -0.5 to 0.5
- attn_gain: bfloat16 [2048], P('dp'), may hold values from 0.099609375 to 1.8984375
- w_gate: bfloat16 [2048, 8192], P('dp', 'tensor'), may hold values from -0.125 to 0.125
- w_up: bfloat16 [2048, 8192], P('dp', 'tensor'), may hold values from -0.125 to 0.125
- w_down: bfloat16 [2048, 8192], P('dp', 'tensor'), may hold values from -0.0625 to 0.0625
- mlp_gain: bfloat16 [2048], P('dp'), may hold values from 0.099609375 to 1.8984375
- cotangent: bfloat16 [16384, 2048], P(('dp', 'tensor')), may hold values from -6 to 6
Outputs:
- block_out: bfloat16 [16384, 2048], P(('dp', 'tensor'))
- grad_tokens: bfloat16 [16384, 2048], P(('dp', 'tensor'))
- grad_query: float32 [2048, 2048], P('dp', 'tensor')
- grad_key: float32 [2048, 2048], P('dp', 'tensor')
- grad_value: float32 [2048, 2048], P('dp', 'tensor')
- grad_output: float32 [2048, 2048], P('dp', 'tensor')
- grad_attn_gain: float32 [2048], P(('dp', 'tensor'))
- grad_gate: float32 [2048, 8192], P('dp', 'tensor')
- grad_up: float32 [2048, 8192], P('dp', 'tensor')
- grad_down: float32 [2048, 8192], P('dp', 'tensor')
- grad_mlp_gain: float32 [2048], P(('dp', 'tensor'))
The draws below stay inside these ranges and needn't reach their ends.
All inputs are finite; a program needn't handle non-finite values.
Results may differ from the reference program's by a relative error of at most 0.018.
Values may be sent and summed in bfloat16 or wider, within the bound.
No kernel may reach another device: no remote copies, remote signals or barrier semaphores. Data moves between devices by JAX's collectives and lax.ppermute only.
A program may use at most 256 MiB of HBM per device.

```python
import jax
import jax.numpy as jnp
from jax import lax

D = 2048
HEADS = 32
HEAD = 64
FF = 8192
LEN = 512
TOKENS = 16384
N_DP = 8


def level_of(rng, shape, pieces, least, largest):
    loudness, own = 1.0, jax.random.fold_in(rng, 6)
    for position, parts in pieces:
        heights = jnp.exp(jax.random.uniform(jax.random.fold_in(own, position), (parts,), jnp.float32, least / len(pieces), largest / len(pieces)))
        loudness = loudness * jnp.repeat(heights, shape[position] // parts).reshape([-1 if axis == position else 1 for axis in range(len(shape))])
    return loudness


def gaussian(stream_key, shape, width, bound, pieces=(), held_as=jnp.bfloat16):
    level = level_of(stream_key, shape, pieces, -0.22, 0.18) if pieces else 1.0
    entries = jax.random.normal(stream_key, shape, jnp.float32) * width * level
    return jnp.minimum(jnp.maximum(entries, -bound), bound).astype(held_as)


def setup_inputs(seed: int = 0) -> dict:
    splits = jax.random.split(jax.random.key(seed), 12)
    return {
        "tokens": gaussian(splits[0], (TOKENS, D), 1.0, 6.0, ((0, 32),)),
        "w_query": gaussian(splits[1], (D, D), D ** -0.5, 0.125, ((0, 8), (1, 4))),
        "w_key": gaussian(splits[2], (D, D), D ** -0.5, 0.125, ((0, 8), (1, 4))),
        "w_value": gaussian(splits[3], (D, D), D ** -0.5, 0.125, ((0, 8), (1, 4))),
        "w_output": gaussian(splits[4], (D, D), (D // 16) ** -0.5, 0.5, ((0, 8), (1, 4))),
        "attn_gain": jnp.clip(1.0 + 0.18 * jax.random.normal(splits[5], (D,), jnp.float32), 0.099609375, 1.8984375).astype(jnp.bfloat16),
        "w_gate": gaussian(splits[6], (D, FF), D ** -0.5, 0.125, ((0, 8), (1, 4))),
        "w_up": gaussian(splits[7], (D, FF), D ** -0.5, 0.125, ((0, 8), (1, 4))),
        "w_down": gaussian(splits[8], (D, FF), FF ** -0.5, 0.0625, ((0, 8), (1, 4))),
        "mlp_gain": jnp.clip(1.0 + 0.18 * jax.random.normal(splits[9], (D,), jnp.float32), 0.099609375, 1.8984375).astype(jnp.bfloat16),
        "cotangent": gaussian(splits[10], (TOKENS, D), 1.0, 6.0, ((0, 32),)),
    }


eps = 1e-05
rope_base = 130000.0

@jax.custom_vjp
def low(v):
    return lax.optimization_barrier(v.astype(jnp.bfloat16)).astype(jnp.float32)

@jax.custom_vjp
def low_back(v):
    return v

def low_keep(v):
    return (low(v), None)

def low_pass(kept, grad):
    return (grad,)

def back_keep(v):
    return (v, None)

def back_low(kept, grad):
    return (low(grad),)
low.defvjp(low_keep, low_pass)
low_back.defvjp(back_keep, back_low)

def matmul(left, right):
    return jnp.dot(left, right, precision=lax.Precision.HIGHEST)

def rms(source, gain):
    inverse = lax.rsqrt(lax.optimization_barrier(jnp.mean(source * source, axis=-1, keepdims=True)) + eps)
    return source * inverse * gain

def tables():
    half = HEAD // 2
    places = jnp.arange(LEN).astype(jnp.float32)
    freqs = rope_base ** (-2.0 * jnp.arange(half).astype(jnp.float32) / HEAD)
    angles = places[:, None] * freqs[None, :]
    return (jnp.cos(angles)[:, None, :], jnp.sin(angles)[:, None, :])

def rotate(values, cosine, sine):
    half = values.shape[-1] // 2
    first = values[..., :half]
    second = values[..., half:]
    return jnp.concatenate([first * cosine - second * sine, second * cosine + first * sine], axis=-1)

def attend(block):
    query_seq, key_seq, value_seq = block
    scores = jnp.einsum('qhd,khd->hqk', query_seq, key_seq, precision=lax.Precision.HIGHEST)
    scores = low_back(scores * HEAD ** (-0.5))
    allowed = jnp.arange(LEN)[:, None] >= jnp.arange(LEN)[None, :]
    scores = jnp.where(allowed[None], scores, -1e+30)
    probs = jax.nn.softmax(scores, axis=-1)
    return jnp.einsum('hqk,khd->qhd', low(probs), value_seq, precision=lax.Precision.HIGHEST)

def layer(source, w_query, w_key, w_value, w_output, attn_gain, w_gate, w_up, w_down, mlp_gain):
    rows = source.shape[0]
    cosine, sine = tables()
    shaped = (rows // LEN, LEN, HEADS, HEAD)
    normed_one = low(rms(source, attn_gain))
    queries = low_back(matmul(normed_one, w_query)).reshape(shaped)
    keys = low_back(matmul(normed_one, w_key)).reshape(shaped)
    values = low(low_back(matmul(normed_one, w_value))).reshape(shaped)
    query_rot = low(rotate(queries, cosine, sine))
    key_rot = low(rotate(keys, cosine, sine))
    attended = lax.map(jax.checkpoint(attend), (query_rot, key_rot, values))
    mixed = low(low_back(attended.reshape(rows, HEADS * HEAD)))
    hidden = source + low_back(matmul(mixed, w_output.T))
    normed_two = low(rms(hidden, mlp_gain))
    gate = low_back(matmul(normed_two, w_gate))
    up = low_back(matmul(normed_two, w_up))
    activ = low(jax.nn.silu(gate) * up)
    return hidden + low_back(matmul(activ, w_down.T))

def reference(tokens, w_query, w_key, w_value, w_output, attn_gain, w_gate, w_up, w_down, mlp_gain, cotangent):
    weights = (w_query.astype(jnp.float32), w_key.astype(jnp.float32), w_value.astype(jnp.float32), w_output.astype(jnp.float32), attn_gain.astype(jnp.float32), w_gate.astype(jnp.float32), w_up.astype(jnp.float32), w_down.astype(jnp.float32), mlp_gain.astype(jnp.float32))
    blocks = tokens.astype(jnp.float32).reshape(N_DP, -1, D)
    grads_in = cotangent.astype(jnp.float32).reshape(N_DP, -1, D)

    def step(totals, block):
        source, grad_out = block
        result, pullback = jax.vjp(layer, source, *weights)
        grads = pullback(grad_out)
        totals = tuple((t + g for t, g in zip(totals, grads[1:])))
        return (totals, (result.astype(jnp.bfloat16), grads[0].astype(jnp.bfloat16)))
    zeros = tuple((jnp.zeros(w.shape, jnp.float32) for w in weights))
    totals, (results, grad_rows) = lax.scan(step, zeros, (blocks, grads_in))
    return (results.reshape(-1, D), grad_rows.reshape(-1, D), totals[0], totals[1], totals[2], totals[3], totals[4], totals[5], totals[6], totals[7], totals[8])
```

```python
import jax
import jax.numpy as jnp
from jax import lax
from jax.experimental import pallas as pl
from jax.experimental.pallas import tpu as pltpu
from jax.sharding import PartitionSpec as P

HEAD = 64
LEN = 512


eps = 1e-05
rope_base = 130000.0


def tables(rows):
    half = HEAD // 2
    places = (jnp.arange(rows) % LEN).astype(jnp.float32)
    freqs = rope_base ** (-2.0 * jnp.arange(half).astype(jnp.float32) / HEAD)
    angles = places[:, None] * freqs[None, :]
    return (jnp.cos(angles)[:, None, :], jnp.sin(angles)[:, None, :])


def rotate(values, cosine, sine):
    half = values.shape[-1] // 2
    first = values[..., :half]
    second = values[..., half:]
    return jnp.concatenate(
        [first * cosine - second * sine, second * cosine + first * sine], axis=-1
    )


def contract_rows(left, right):
    return lax.dot_general(
        left, right, (((0,), (0,)), ((), ())), preferred_element_type=jnp.float32
    )


def contract_cols(left, right):
    return lax.dot_general(
        left, right, (((1,), (1,)), ((), ())), preferred_element_type=jnp.float32
    )


def causal_scores(query_seq, key_seq):
    scores = jnp.einsum("qhd,khd->hqk", query_seq, key_seq, preferred_element_type=jnp.float32)
    scores = scores * HEAD ** (-0.5)
    length = query_seq.shape[0]
    allowed = jnp.arange(length)[:, None] >= jnp.arange(length)[None, :]
    return jnp.where(allowed[None], scores, -1e30)


def attend_forward(block):
    query_seq, key_seq, value_seq = block
    scores = causal_scores(query_seq, key_seq)
    top = jnp.max(scores, axis=-1, keepdims=True)
    expo = jnp.exp(scores - top)
    total = jnp.sum(expo, axis=-1, keepdims=True)
    probs = (expo / total).astype(jnp.bfloat16)
    attended = jnp.einsum("hqk,khd->qhd", probs, value_seq, preferred_element_type=jnp.float32)
    return (attended, top + jnp.log(total))


def attend_backward(block):
    query_seq, key_seq, value_seq, log_total, grad_seq = block
    scores = causal_scores(query_seq, key_seq)
    probs = jnp.exp(scores - log_total)
    grad_probs = jnp.einsum("qhd,khd->hqk", grad_seq, value_seq, preferred_element_type=jnp.float32)
    inner = jnp.sum(probs * grad_probs, axis=-1, keepdims=True)
    grad_scores = (probs * (grad_probs - inner)).astype(jnp.bfloat16)
    factor = HEAD ** (-0.5)
    grad_query = (
        jnp.einsum("hqk,khd->qhd", grad_scores, key_seq, preferred_element_type=jnp.float32)
        * factor
    )
    grad_key = (
        jnp.einsum("hqk,qhd->khd", grad_scores, query_seq, preferred_element_type=jnp.float32)
        * factor
    )
    grad_value = jnp.einsum(
        "hqk,qhd->khd", probs.astype(jnp.bfloat16), grad_seq, preferred_element_type=jnp.float32
    )
    return (grad_query, grad_key, grad_value)


def norm_back(grad_normed, source, inverse, gain):
    scaled = grad_normed * gain
    inner = jnp.mean(scaled * source, axis=-1, keepdims=True)
    grad_source = inverse * scaled - source * inverse**3 * inner
    grad_gain = jnp.sum(grad_normed * source * inverse, axis=0)
    return (grad_source, grad_gain)


def tensor_parallel(
    tokens, w_query, w_key, w_value, w_output, attn_gain, w_gate, w_up, w_down, mlp_gain, cotangent
):
    query_full, key_full, value_full, output_full, attn_scale = (
        lax.all_gather(w_query, "dp", axis=0, tiled=True),
        lax.all_gather(w_key, "dp", axis=0, tiled=True),
        lax.all_gather(w_value, "dp", axis=0, tiled=True),
        lax.all_gather(w_output, "dp", axis=0, tiled=True),
        lax.all_gather(attn_gain, "dp", axis=0, tiled=True),
    )
    gate_full, up_full, down_full, mlp_scale = (
        lax.all_gather(w_gate, "dp", axis=0, tiled=True),
        lax.all_gather(w_up, "dp", axis=0, tiled=True),
        lax.all_gather(w_down, "dp", axis=0, tiled=True),
        lax.all_gather(mlp_gain, "dp", axis=0, tiled=True),
    )
    attn_scale = attn_scale.astype(jnp.float32)
    mlp_scale = mlp_scale.astype(jnp.float32)
    source = tokens.astype(jnp.float32)
    inverse_one = lax.rsqrt(jnp.mean(source * source, axis=-1, keepdims=True) + eps)
    normed_one = (source * inverse_one * attn_scale).astype(jnp.bfloat16)
    gathered_one = lax.all_gather(normed_one, "tensor", axis=0, tiled=True)
    rows = gathered_one.shape[0]
    local_heads = query_full.shape[1] // HEAD
    seq_count = rows // LEN
    cosine, sine = tables(rows)

    def by_seq(values):
        return values.reshape(seq_count, LEN, local_heads, HEAD)

    queries = jnp.dot(gathered_one, query_full, preferred_element_type=jnp.float32).reshape(
        rows, local_heads, HEAD
    )
    keys = jnp.dot(gathered_one, key_full, preferred_element_type=jnp.float32).reshape(
        rows, local_heads, HEAD
    )
    values = jnp.dot(gathered_one, value_full, preferred_element_type=jnp.float32).astype(
        jnp.bfloat16
    )
    query_rot = rotate(queries, cosine, sine).astype(jnp.bfloat16)
    key_rot = rotate(keys, cosine, sine).astype(jnp.bfloat16)
    attended, log_total = lax.map(
        attend_forward, (by_seq(query_rot), by_seq(key_rot), by_seq(values))
    )
    mixed_heads = attended.reshape(rows, local_heads * HEAD).astype(jnp.bfloat16)
    part = mixed_heads
    attn_branch = lax.psum_scatter(
        contract_cols(part, output_full), "tensor", scatter_dimension=0, tiled=True
    )
    hidden = source + attn_branch
    inverse_two = lax.rsqrt(jnp.mean(hidden * hidden, axis=-1, keepdims=True) + eps)
    normed_two = (hidden * inverse_two * mlp_scale).astype(jnp.bfloat16)
    gathered_two = lax.all_gather(normed_two, "tensor", axis=0, tiled=True)
    gate = jnp.dot(gathered_two, gate_full, preferred_element_type=jnp.float32)
    up = jnp.dot(gathered_two, up_full, preferred_element_type=jnp.float32)
    sigma = jax.nn.sigmoid(gate)
    swish = gate * sigma
    activ = (swish * up).astype(jnp.bfloat16)
    part = activ
    mlp_branch = lax.psum_scatter(
        contract_cols(part, down_full).astype(jnp.bfloat16),
        "tensor",
        scatter_dimension=0,
        tiled=True,
    ).astype(jnp.float32)
    block_out = (hidden + mlp_branch).astype(jnp.bfloat16)
    gate_back, up_back, down_back = (
        lax.all_gather(w_gate, "dp", axis=0, tiled=True),
        lax.all_gather(w_up, "dp", axis=0, tiled=True),
        lax.all_gather(w_down, "dp", axis=0, tiled=True),
    )
    grad_out_rows = lax.all_gather(cotangent, "tensor", axis=0, tiled=True)
    grad_activ = jnp.dot(grad_out_rows, down_back, preferred_element_type=jnp.float32)
    grad_gate_pre = (grad_activ * up * sigma * (1.0 + gate * (1.0 - sigma))).astype(jnp.bfloat16)
    grad_up_pre = (grad_activ * swish).astype(jnp.bfloat16)
    grad_down_w = contract_rows(grad_out_rows, activ)
    grad_gate_w = contract_rows(gathered_two, grad_gate_pre)
    grad_up_w = contract_rows(gathered_two, grad_up_pre)
    grad_normed_two = lax.psum_scatter(
        contract_cols(grad_gate_pre, gate_back) + contract_cols(grad_up_pre, up_back),
        "tensor",
        scatter_dimension=0,
        tiled=True,
    )
    grad_hidden_norm, grad_mlp_gain = norm_back(grad_normed_two, hidden, inverse_two, mlp_scale)
    grad_hidden = cotangent.astype(jnp.float32) + grad_hidden_norm
    grad_branch = grad_hidden.astype(jnp.bfloat16)
    grad_branch_rows = lax.all_gather(grad_branch, "tensor", axis=0, tiled=True)
    grad_mixed = jnp.dot(grad_branch_rows, output_full, preferred_element_type=jnp.float32).astype(
        jnp.bfloat16
    )
    grad_output_w = contract_rows(grad_branch_rows, mixed_heads)
    grad_query_rot, grad_key_rot, grad_value_seq = lax.map(
        attend_backward,
        (by_seq(query_rot), by_seq(key_rot), by_seq(values), log_total, by_seq(grad_mixed)),
    )
    grad_q_pre = rotate(grad_query_rot.reshape(rows, local_heads, HEAD), cosine, -sine)
    grad_q_pre = grad_q_pre.reshape(rows, local_heads * HEAD).astype(jnp.bfloat16)
    grad_k_pre = rotate(grad_key_rot.reshape(rows, local_heads, HEAD), cosine, -sine)
    grad_k_pre = grad_k_pre.reshape(rows, local_heads * HEAD).astype(jnp.bfloat16)
    grad_v_pre = grad_value_seq.reshape(rows, local_heads * HEAD).astype(jnp.bfloat16)
    grad_query_w = contract_rows(gathered_one, grad_q_pre)
    grad_key_w = contract_rows(gathered_one, grad_k_pre)
    grad_value_w = contract_rows(gathered_one, grad_v_pre)
    total = contract_cols(grad_q_pre, query_full) + contract_cols(grad_k_pre, key_full)
    grad_normed_one = lax.psum_scatter(
        (total + contract_cols(grad_v_pre, value_full)).astype(jnp.bfloat16),
        "tensor",
        scatter_dimension=0,
        tiled=True,
    ).astype(jnp.float32)
    grad_source_norm, grad_attn_gain = norm_back(grad_normed_one, source, inverse_one, attn_scale)
    grad_tokens = (grad_hidden + grad_source_norm).astype(jnp.bfloat16)
    grad_query, grad_key, grad_value, grad_output = (
        lax.psum_scatter(
            grad_query_w.astype(jnp.bfloat16), "dp", scatter_dimension=0, tiled=True
        ).astype(jnp.float32),
        lax.psum_scatter(
            grad_key_w.astype(jnp.bfloat16), "dp", scatter_dimension=0, tiled=True
        ).astype(jnp.float32),
        lax.psum_scatter(
            grad_value_w.astype(jnp.bfloat16), "dp", scatter_dimension=0, tiled=True
        ).astype(jnp.float32),
        lax.psum_scatter(
            grad_output_w.astype(jnp.bfloat16), "dp", scatter_dimension=0, tiled=True
        ).astype(jnp.float32),
    )
    grad_gate, grad_up, grad_down = (
        lax.psum_scatter(
            grad_gate_w.astype(jnp.bfloat16), "dp", scatter_dimension=0, tiled=True
        ).astype(jnp.float32),
        lax.psum_scatter(
            grad_up_w.astype(jnp.bfloat16), "dp", scatter_dimension=0, tiled=True
        ).astype(jnp.float32),
        lax.psum_scatter(
            grad_down_w.astype(jnp.bfloat16), "dp", scatter_dimension=0, tiled=True
        ).astype(jnp.float32),
    )
    attn_gain_sum, mlp_gain_sum = (
        lax.psum_scatter(grad_attn_gain, ("dp", "tensor"), scatter_dimension=0, tiled=True),
        lax.psum_scatter(grad_mlp_gain, ("dp", "tensor"), scatter_dimension=0, tiled=True),
    )
    return (
        block_out,
        grad_tokens,
        grad_query,
        grad_key,
        grad_value,
        grad_output,
        attn_gain_sum,
        grad_gate,
        grad_up,
        grad_down,
        mlp_gain_sum,
    )


PAIR = 2 * HEAD


def lane_tables():
    half = HEAD // 2
    lanes = jnp.arange(PAIR)
    freqs = rope_base ** (-2.0 * (lanes % half).astype(jnp.float32) / HEAD)
    angles = jnp.arange(LEN).astype(jnp.float32)[:, None] * freqs[None, :]
    signs = jnp.where(lanes % HEAD < half, -1.0, 1.0)
    return (jnp.cos(angles), jnp.sin(angles) * signs[None, :])


def swap_halves(values, lanes):
    half = HEAD // 2
    return jnp.where(
        lanes % HEAD < half,
        pltpu.roll(values, PAIR - half, 1),
        pltpu.roll(values, half, 1),
    )


def dot_last(left, right):
    return lax.dot_general(
        left, right, (((1,), (1,)), ((), ())), preferred_element_type=jnp.float32
    )


def dot_first(left, right):
    return lax.dot_general(
        left, right, (((0,), (0,)), ((), ())), preferred_element_type=jnp.float32
    )


def forward_kernel(q_ref, k_ref, v_ref, cos_ref, sin_ref, qr_ref, kr_ref, vb_ref, mix_ref):
    lanes = lax.broadcasted_iota(jnp.int32, (LEN, PAIR), 1)
    cosine = cos_ref[...]
    sine = sin_ref[...]

    def rotated(values):
        return (values * cosine + swap_halves(values, lanes) * sine).astype(jnp.bfloat16)

    query = rotated(q_ref[...])
    key = rotated(k_ref[...])
    value = v_ref[...].astype(jnp.bfloat16)
    qr_ref[...] = query
    kr_ref[...] = key
    vb_ref[...] = value
    scaled = query * jnp.bfloat16(HEAD**-0.5)
    step = LEN // 2
    for part in range(2):
        rows = slice(part * step, (part + 1) * step)
        seen = (part + 1) * step
        shape = (step, seen)
        allowed = lax.broadcasted_iota(jnp.int32, shape, 0) + part * step >= (
            lax.broadcasted_iota(jnp.int32, shape, 1)
        )
        mixed = []
        for head in range(2):
            mine = lanes[rows] // HEAD == head
            one_head = jnp.where(mine, scaled[rows], jnp.zeros_like(scaled[rows]))
            scores = jnp.where(allowed, dot_last(one_head, key[:seen]), -1e30)
            top = jnp.max(scores, axis=-1, keepdims=True)
            expo = jnp.exp(scores - top)
            total = jnp.sum(expo, axis=-1, keepdims=True)
            probs = (expo * (1.0 / total)).astype(jnp.bfloat16)
            mixed.append(jnp.dot(probs, value[:seen], preferred_element_type=jnp.float32))
        both = jnp.where(lanes[rows] < HEAD, mixed[0], mixed[1])
        mix_ref[rows, :] = both.astype(jnp.bfloat16)


def backward_kernel(q_ref, k_ref, v_ref, g_ref, cos_ref, sin_ref, out_ref):
    lanes = lax.broadcasted_iota(jnp.int32, (LEN, PAIR), 1)
    cosine = cos_ref[...]
    sine = sin_ref[...]
    factor = jnp.bfloat16(HEAD**-0.5)
    query = q_ref[...] * factor
    key = k_ref[...]
    key_scaled = key * factor
    value = v_ref[...]
    grad = g_ref[...]
    step = LEN // 2
    grad_query, grad_key, grad_value = [], [], []
    for part in range(2):
        rows = slice(part * step, (part + 1) * step)
        seen = (part + 1) * step
        shape = (seen, step)
        allowed = lax.broadcasted_iota(jnp.int32, shape, 1) + part * step >= (
            lax.broadcasted_iota(jnp.int32, shape, 0)
        )
        for head in range(2):
            mine = lanes[rows] // HEAD == head
            own = lanes[:seen] // HEAD == head
            q_one = jnp.where(mine, query[rows], jnp.zeros_like(query[rows]))
            g_one = jnp.where(mine, grad[rows], jnp.zeros_like(grad[rows]))
            k_one = jnp.where(own, key_scaled[:seen], jnp.zeros_like(key[:seen]))
            scores = jnp.where(allowed, dot_last(key[:seen], q_one), -1e30)
            top = jnp.max(scores, axis=0, keepdims=True)
            expo = jnp.exp(scores - top)
            total = jnp.sum(expo, axis=0, keepdims=True)
            probs = expo * (1.0 / total)
            grad_probs = dot_last(value[:seen], g_one)
            inner = jnp.sum(probs * grad_probs, axis=0, keepdims=True)
            grad_scores = (probs * (grad_probs - inner)).astype(jnp.bfloat16)
            rounded = probs.astype(jnp.bfloat16)
            grad_value.append(jnp.dot(rounded, g_one, preferred_element_type=jnp.float32))
            grad_key.append(jnp.dot(grad_scores, q_one, preferred_element_type=jnp.float32))
            grad_query.append(dot_first(grad_scores, k_one))

    def gather(parts):
        first = parts[0] + parts[1]
        second = parts[2] + parts[3]
        return jnp.concatenate([first + second[:step], second[step:]], axis=0)

    def unrotated(values):
        return (values * cosine - swap_halves(values, lanes) * sine).astype(jnp.bfloat16)

    all_query = jnp.concatenate(
        [grad_query[0] + grad_query[1], grad_query[2] + grad_query[3]], axis=0
    )
    columns = out_ref.shape[1] // 3
    place = pl.multiple_of(pl.program_id(0) * PAIR, PAIR)
    out_ref[:, pl.ds(place, PAIR)] = unrotated(all_query)
    out_ref[:, pl.ds(columns + place, PAIR)] = unrotated(gather(grad_key))
    out_ref[:, pl.ds(2 * columns + place, PAIR)] = gather(grad_value).astype(jnp.bfloat16)


def pair_block(offset):
    return pl.BlockSpec((LEN, PAIR), lambda step: (0, offset + step))


def whole_block(columns):
    return pl.BlockSpec((LEN, columns), lambda step: (0, 0))


def attention(qkv, cosine, sine):
    columns = qkv.shape[1] // 3
    pairs = columns // PAIR
    flat = jax.ShapeDtypeStruct((LEN, columns), jnp.bfloat16)
    return pl.pallas_call(
        forward_kernel,
        grid=(pairs,),
        in_specs=[pair_block(0), pair_block(pairs), pair_block(2 * pairs)]
        + [whole_block(PAIR)] * 2,
        out_specs=[pair_block(0)] * 4,
        out_shape=[flat] * 4,
        name="attend",
        cost_estimate=pl.CostEstimate(
            flops=8 * LEN * LEN * columns,
            transcendentals=LEN * LEN * columns // HEAD,
            bytes_accessed=20 * LEN * columns,
        ),
    )(qkv, qkv, qkv, cosine, sine)


def attention_back(query, key, value, grad, cosine, sine):
    columns = query.shape[1]
    return pl.pallas_call(
        backward_kernel,
        grid=(columns // PAIR,),
        in_specs=[pair_block(0)] * 4 + [whole_block(PAIR)] * 2,
        out_specs=whole_block(3 * columns),
        out_shape=jax.ShapeDtypeStruct((LEN, 3 * columns), jnp.bfloat16),
        name="attend_back",
        cost_estimate=pl.CostEstimate(
            flops=20 * LEN * LEN * columns,
            transcendentals=LEN * LEN * columns // HEAD,
            bytes_accessed=14 * LEN * columns,
        ),
    )(query, key, value, grad, cosine, sine)


def shift(values, count):
    return lax.ppermute(values, "tensor", [(i, (i + 1) % count) for i in range(count)])


def travel(values, count):
    stops = [values]
    for _ in range(count - 1):
        stops.append(shift(stops[-1], count))
    return stops


def ring_sum(parts, count):
    total = parts[1]
    for j in list(range(2, count)) + [0]:
        total = shift(total.astype(jnp.bfloat16), count).astype(jnp.float32) + parts[j]
    return total


def sum_all(values, axes):
    for name, count in axes:
        hop = 1
        while hop < count:
            values = values + lax.ppermute(values, name, [(i, i ^ hop) for i in range(count)])
            hop *= 2
    return values


def token_parallel(
    tokens, w_query, w_key, w_value, w_output, attn_gain, w_gate, w_up, w_down, mlp_gain, cotangent
):
    count = lax.axis_size("tensor")
    dp_count = lax.axis_size("dp")
    heads = w_query.shape[1]
    hidden_units = w_gate.shape[1]
    gains = lax.all_gather(jnp.stack([attn_gain, mlp_gain]), "dp", axis=0)
    gains = jnp.swapaxes(gains, 0, 1).reshape(2, -1).astype(jnp.float32)
    attn_scale, mlp_scale = gains[0], gains[1]
    shard = jnp.concatenate([w_query, w_key, w_value, w_output], axis=1)
    own = lax.all_gather(shard, "dp", axis=0, tiled=True)
    others = travel(shard, count)[1:]
    rest_shard = jnp.concatenate(
        [other[:, k * heads : (k + 1) * heads] for k in range(4) for other in others], axis=1
    )
    rest = lax.all_gather(rest_shard, "dp", axis=0, tiled=True)
    wide = (count - 1) * heads
    gate_up = lax.all_gather(jnp.concatenate([w_gate, w_up], axis=1), "dp", axis=0, tiled=True)
    down = lax.all_gather(w_down, "dp", axis=0, tiled=True)
    cotangents = travel(cotangent, count)

    source = tokens.astype(jnp.float32)
    inverse_one = lax.rsqrt(jnp.mean(source * source, axis=-1, keepdims=True) + eps)
    normed_one = (source * inverse_one * attn_scale).astype(jnp.bfloat16)
    cosine, sine = lane_tables()
    own_qkv = jnp.dot(normed_one, own[:, : 3 * heads], preferred_element_type=jnp.float32)
    own_query, own_key, own_value, own_mixed = attention(own_qkv, cosine, sine)
    rest_qkv = jnp.dot(normed_one, rest[:, : 3 * wide], preferred_element_type=jnp.float32)
    rest_query, rest_key, rest_value, rest_mixed = attention(rest_qkv, cosine, sine)
    branch = contract_cols(own_mixed, own[:, 3 * heads :])
    branch = branch + contract_cols(rest_mixed, rest[:, 3 * wide :])
    hidden = source + branch
    inverse_two = lax.rsqrt(jnp.mean(hidden * hidden, axis=-1, keepdims=True) + eps)
    normed_two = (hidden * inverse_two * mlp_scale).astype(jnp.bfloat16)

    normed = travel(normed_two, count)
    activs, pres, mlp_parts, norm_parts = [], [], [], []
    for normed_rows, grad_rows in zip(normed, cotangents):
        both = jnp.dot(normed_rows, gate_up, preferred_element_type=jnp.float32)
        gate, up = both[:, :hidden_units], both[:, hidden_units:]
        sigma = jax.nn.sigmoid(gate)
        swish = gate * sigma
        activ = (swish * up).astype(jnp.bfloat16)
        grad_activ = jnp.dot(grad_rows, down, preferred_element_type=jnp.float32)
        grad_gate_pre = (grad_activ * up * sigma * (1.0 + gate * (1.0 - sigma))).astype(
            jnp.bfloat16
        )
        grad_up_pre = (grad_activ * swish).astype(jnp.bfloat16)
        pre = jnp.concatenate([grad_gate_pre, grad_up_pre], axis=1)
        activs.append(activ)
        pres.append(pre)
        norm_parts.append(contract_cols(pre, gate_up))
        mlp_parts.append(contract_cols(activ, down))
    grad_normed_two = ring_sum(norm_parts, count)
    mlp_branch = ring_sum(mlp_parts, count)
    block_out = (hidden + mlp_branch).astype(jnp.bfloat16)
    all_normed = jnp.concatenate(normed, axis=0)
    all_cotangents = jnp.concatenate(cotangents, axis=0)
    grad_gate_up_w = contract_rows(all_normed, jnp.concatenate(pres, axis=0)).astype(jnp.bfloat16)
    grad_down_w = contract_rows(all_cotangents, jnp.concatenate(activs, axis=0)).astype(
        jnp.bfloat16
    )

    def over_dp(values):
        return lax.psum_scatter(values, "dp", scatter_dimension=0, tiled=True)

    grad_gate_up = over_dp(grad_gate_up_w).astype(jnp.float32)
    grad_down = over_dp(grad_down_w).astype(jnp.float32)

    grad_hidden_norm, mlp_gain_part = norm_back(grad_normed_two, hidden, inverse_two, mlp_scale)
    grad_hidden = cotangent.astype(jnp.float32) + grad_hidden_norm
    grad_branch = grad_hidden.astype(jnp.bfloat16)
    all_mixed = jnp.concatenate([own_mixed, rest_mixed], axis=1)
    grad_output_w = contract_rows(grad_branch, all_mixed).astype(jnp.bfloat16)
    rest_grad = jnp.dot(
        grad_branch, rest[:, 3 * wide :], preferred_element_type=jnp.float32
    ).astype(jnp.bfloat16)
    own_grad = jnp.dot(
        grad_branch, own[:, 3 * heads :], preferred_element_type=jnp.float32
    ).astype(jnp.bfloat16)
    rest_pre = attention_back(rest_query, rest_key, rest_value, rest_grad, cosine, sine)
    rest_grad_w = contract_rows(normed_one, rest_pre).astype(jnp.bfloat16)
    own_pre = attention_back(own_query, own_key, own_value, own_grad, cosine, sine)
    own_grad_w = contract_rows(normed_one, own_pre).astype(jnp.bfloat16)
    grad_normed_one = contract_cols(rest_pre, rest[:, : 3 * wide])
    grad_normed_one = grad_normed_one + contract_cols(own_pre, own[:, : 3 * heads])
    grad_source_norm, attn_gain_part = norm_back(grad_normed_one, source, inverse_one, attn_scale)
    grad_tokens = (grad_hidden + grad_source_norm).astype(jnp.bfloat16)

    output_sum = over_dp(grad_output_w)
    rest_sum = over_dp(rest_grad_w)
    own_sum = over_dp(own_grad_w)
    slots = [jnp.concatenate([own_sum, output_sum[:, :heads]], axis=1)]
    for j in range(1, count):
        columns = [rest_sum[:, k * wide + (j - 1) * heads : k * wide + j * heads] for k in range(3)]
        slots.append(jnp.concatenate(columns + [output_sum[:, j * heads : (j + 1) * heads]], axis=1))
    grads = ring_sum([slot.astype(jnp.float32) for slot in slots], count)
    grad_query, grad_key, grad_value, grad_output = [
        grads[:, k * heads : (k + 1) * heads] for k in range(4)
    ]
    gain_parts = sum_all(
        jnp.stack([attn_gain_part, mlp_gain_part]), (("dp", dp_count), ("tensor", count))
    )
    piece = gain_parts.shape[1] // (dp_count * count)
    place = (lax.axis_index("dp") * count + lax.axis_index("tensor")) * piece
    gain_sums = lax.dynamic_slice_in_dim(gain_parts, place, piece, axis=1)
    return (
        block_out,
        grad_tokens,
        grad_query,
        grad_key,
        grad_value,
        grad_output,
        gain_sums[0],
        grad_gate_up[:, :hidden_units],
        grad_gate_up[:, hidden_units:],
        grad_down,
        gain_sums[1],
    )


def power_of_two(number):
    return number & (number - 1) == 0


def local(tokens, w_query, *others):
    axes = (lax.axis_size("dp"), lax.axis_size("tensor"))
    whole = tokens.shape[0] == LEN and w_query.shape[1] % PAIR == 0
    if whole and axes[1] > 1 and all(power_of_two(size) for size in axes):
        return token_parallel(tokens, w_query, *others)
    return tensor_parallel(tokens, w_query, *others)


def solution(mesh):
    in_specs = (
        P(("dp", "tensor"), None),
        P("dp", "tensor"),
        P("dp", "tensor"),
        P("dp", "tensor"),
        P("dp", "tensor"),
        P("dp"),
        P("dp", "tensor"),
        P("dp", "tensor"),
        P("dp", "tensor"),
        P("dp"),
        P(("dp", "tensor"), None),
    )
    out_specs = (
        P(("dp", "tensor"), None),
        P(("dp", "tensor"), None),
        P("dp", "tensor"),
        P("dp", "tensor"),
        P("dp", "tensor"),
        P("dp", "tensor"),
        P(("dp", "tensor")),
        P("dp", "tensor"),
        P("dp", "tensor"),
        P("dp", "tensor"),
        P(("dp", "tensor")),
    )
    return jax.shard_map(local, mesh=mesh, in_specs=in_specs, out_specs=out_specs, check_vma=False)
```

```python
import jax
import jax.numpy as jnp
from jax import lax
from jax.experimental import pallas as pl
from jax.experimental.pallas import tpu as pltpu
from jax.sharding import PartitionSpec as P

HEAD = 64
LEN = 512


eps = 1e-05
rope_base = 130000.0


def tables(rows):
    half = HEAD // 2
    places = (jnp.arange(rows) % LEN).astype(jnp.float32)
    freqs = rope_base ** (-2.0 * jnp.arange(half).astype(jnp.float32) / HEAD)
    angles = places[:, None] * freqs[None, :]
    return (jnp.cos(angles)[:, None, :], jnp.sin(angles)[:, None, :])


def rotate(values, cosine, sine):
    half = values.shape[-1] // 2
    first = values[..., :half]
    second = values[..., half:]
    return jnp.concatenate(
        [first * cosine - second * sine, second * cosine + first * sine], axis=-1
    )


def contract_rows(left, right):
    return lax.dot_general(
        left, right, (((0,), (0,)), ((), ())), preferred_element_type=jnp.float32
    )


def contract_cols(left, right):
    return lax.dot_general(
        left, right, (((1,), (1,)), ((), ())), preferred_element_type=jnp.float32
    )


def causal_scores(query_seq, key_seq):
    scores = jnp.einsum("qhd,khd->hqk", query_seq, key_seq, preferred_element_type=jnp.float32)
    scores = scores * HEAD ** (-0.5)
    length = query_seq.shape[0]
    allowed = jnp.arange(length)[:, None] >= jnp.arange(length)[None, :]
    return jnp.where(allowed[None], scores, -1e30)


def attend_forward(block):
    query_seq, key_seq, value_seq = block
    scores = causal_scores(query_seq, key_seq)
    top = jnp.max(scores, axis=-1, keepdims=True)
    expo = jnp.exp(scores - top)
    total = jnp.sum(expo, axis=-1, keepdims=True)
    probs = (expo / total).astype(jnp.bfloat16)
    attended = jnp.einsum("hqk,khd->qhd", probs, value_seq, preferred_element_type=jnp.float32)
    return (attended, top + jnp.log(total))


def attend_backward(block):
    query_seq, key_seq, value_seq, log_total, grad_seq = block
    scores = causal_scores(query_seq, key_seq)
    probs = jnp.exp(scores - log_total)
    grad_probs = jnp.einsum("qhd,khd->hqk", grad_seq, value_seq, preferred_element_type=jnp.float32)
    inner = jnp.sum(probs * grad_probs, axis=-1, keepdims=True)
    grad_scores = (probs * (grad_probs - inner)).astype(jnp.bfloat16)
    factor = HEAD ** (-0.5)
    grad_query = (
        jnp.einsum("hqk,khd->qhd", grad_scores, key_seq, preferred_element_type=jnp.float32)
        * factor
    )
    grad_key = (
        jnp.einsum("hqk,qhd->khd", grad_scores, query_seq, preferred_element_type=jnp.float32)
        * factor
    )
    grad_value = jnp.einsum(
        "hqk,qhd->khd", probs.astype(jnp.bfloat16), grad_seq, preferred_element_type=jnp.float32
    )
    return (grad_query, grad_key, grad_value)


def norm_back(grad_normed, source, inverse, gain):
    scaled = grad_normed * gain
    inner = jnp.mean(scaled * source, axis=-1, keepdims=True)
    grad_source = inverse * scaled - source * inverse**3 * inner
    grad_gain = jnp.sum(grad_normed * source * inverse, axis=0)
    return (grad_source, grad_gain)


def tensor_parallel(
    tokens, w_query, w_key, w_value, w_output, attn_gain, w_gate, w_up, w_down, mlp_gain, cotangent
):
    query_full, key_full, value_full, output_full, attn_scale = (
        lax.all_gather(w_query, "dp", axis=0, tiled=True),
        lax.all_gather(w_key, "dp", axis=0, tiled=True),
        lax.all_gather(w_value, "dp", axis=0, tiled=True),
        lax.all_gather(w_output, "dp", axis=0, tiled=True),
        lax.all_gather(attn_gain, "dp", axis=0, tiled=True),
    )
    gate_full, up_full, down_full, mlp_scale = (
        lax.all_gather(w_gate, "dp", axis=0, tiled=True),
        lax.all_gather(w_up, "dp", axis=0, tiled=True),
        lax.all_gather(w_down, "dp", axis=0, tiled=True),
        lax.all_gather(mlp_gain, "dp", axis=0, tiled=True),
    )
    attn_scale = attn_scale.astype(jnp.float32)
    mlp_scale = mlp_scale.astype(jnp.float32)
    source = tokens.astype(jnp.float32)
    inverse_one = lax.rsqrt(jnp.mean(source * source, axis=-1, keepdims=True) + eps)
    normed_one = (source * inverse_one * attn_scale).astype(jnp.bfloat16)
    gathered_one = lax.all_gather(normed_one, "tensor", axis=0, tiled=True)
    rows = gathered_one.shape[0]
    local_heads = query_full.shape[1] // HEAD
    seq_count = rows // LEN
    cosine, sine = tables(rows)

    def by_seq(values):
        return values.reshape(seq_count, LEN, local_heads, HEAD)

    queries = jnp.dot(gathered_one, query_full, preferred_element_type=jnp.float32).reshape(
        rows, local_heads, HEAD
    )
    keys = jnp.dot(gathered_one, key_full, preferred_element_type=jnp.float32).reshape(
        rows, local_heads, HEAD
    )
    values = jnp.dot(gathered_one, value_full, preferred_element_type=jnp.float32).astype(
        jnp.bfloat16
    )
    query_rot = rotate(queries, cosine, sine).astype(jnp.bfloat16)
    key_rot = rotate(keys, cosine, sine).astype(jnp.bfloat16)
    attended, log_total = lax.map(
        attend_forward, (by_seq(query_rot), by_seq(key_rot), by_seq(values))
    )
    mixed_heads = attended.reshape(rows, local_heads * HEAD).astype(jnp.bfloat16)
    part = mixed_heads
    attn_branch = lax.psum_scatter(
        contract_cols(part, output_full), "tensor", scatter_dimension=0, tiled=True
    )
    hidden = source + attn_branch
    inverse_two = lax.rsqrt(jnp.mean(hidden * hidden, axis=-1, keepdims=True) + eps)
    normed_two = (hidden * inverse_two * mlp_scale).astype(jnp.bfloat16)
    gathered_two = lax.all_gather(normed_two, "tensor", axis=0, tiled=True)
    gate = jnp.dot(gathered_two, gate_full, preferred_element_type=jnp.float32)
    up = jnp.dot(gathered_two, up_full, preferred_element_type=jnp.float32)
    sigma = jax.nn.sigmoid(gate)
    swish = gate * sigma
    activ = (swish * up).astype(jnp.bfloat16)
    part = activ
    mlp_branch = lax.psum_scatter(
        contract_cols(part, down_full).astype(jnp.bfloat16),
        "tensor",
        scatter_dimension=0,
        tiled=True,
    ).astype(jnp.float32)
    block_out = (hidden + mlp_branch).astype(jnp.bfloat16)
    gate_back, up_back, down_back = (
        lax.all_gather(w_gate, "dp", axis=0, tiled=True),
        lax.all_gather(w_up, "dp", axis=0, tiled=True),
        lax.all_gather(w_down, "dp", axis=0, tiled=True),
    )
    grad_out_rows = lax.all_gather(cotangent, "tensor", axis=0, tiled=True)
    grad_activ = jnp.dot(grad_out_rows, down_back, preferred_element_type=jnp.float32)
    grad_gate_pre = (grad_activ * up * sigma * (1.0 + gate * (1.0 - sigma))).astype(jnp.bfloat16)
    grad_up_pre = (grad_activ * swish).astype(jnp.bfloat16)
    grad_down_w = contract_rows(grad_out_rows, activ)
    grad_gate_w = contract_rows(gathered_two, grad_gate_pre)
    grad_up_w = contract_rows(gathered_two, grad_up_pre)
    grad_normed_two = lax.psum_scatter(
        contract_cols(grad_gate_pre, gate_back) + contract_cols(grad_up_pre, up_back),
        "tensor",
        scatter_dimension=0,
        tiled=True,
    )
    grad_hidden_norm, grad_mlp_gain = norm_back(grad_normed_two, hidden, inverse_two, mlp_scale)
    grad_hidden = cotangent.astype(jnp.float32) + grad_hidden_norm
    grad_branch = grad_hidden.astype(jnp.bfloat16)
    grad_branch_rows = lax.all_gather(grad_branch, "tensor", axis=0, tiled=True)
    grad_mixed = jnp.dot(grad_branch_rows, output_full, preferred_element_type=jnp.float32).astype(
        jnp.bfloat16
    )
    grad_output_w = contract_rows(grad_branch_rows, mixed_heads)
    grad_query_rot, grad_key_rot, grad_value_seq = lax.map(
        attend_backward,
        (by_seq(query_rot), by_seq(key_rot), by_seq(values), log_total, by_seq(grad_mixed)),
    )
    grad_q_pre = rotate(grad_query_rot.reshape(rows, local_heads, HEAD), cosine, -sine)
    grad_q_pre = grad_q_pre.reshape(rows, local_heads * HEAD).astype(jnp.bfloat16)
    grad_k_pre = rotate(grad_key_rot.reshape(rows, local_heads, HEAD), cosine, -sine)
    grad_k_pre = grad_k_pre.reshape(rows, local_heads * HEAD).astype(jnp.bfloat16)
    grad_v_pre = grad_value_seq.reshape(rows, local_heads * HEAD).astype(jnp.bfloat16)
    grad_query_w = contract_rows(gathered_one, grad_q_pre)
    grad_key_w = contract_rows(gathered_one, grad_k_pre)
    grad_value_w = contract_rows(gathered_one, grad_v_pre)
    total = contract_cols(grad_q_pre, query_full) + contract_cols(grad_k_pre, key_full)
    grad_normed_one = lax.psum_scatter(
        (total + contract_cols(grad_v_pre, value_full)).astype(jnp.bfloat16),
        "tensor",
        scatter_dimension=0,
        tiled=True,
    ).astype(jnp.float32)
    grad_source_norm, grad_attn_gain = norm_back(grad_normed_one, source, inverse_one, attn_scale)
    grad_tokens = (grad_hidden + grad_source_norm).astype(jnp.bfloat16)
    grad_query, grad_key, grad_value, grad_output = (
        lax.psum_scatter(
            grad_query_w.astype(jnp.bfloat16), "dp", scatter_dimension=0, tiled=True
        ).astype(jnp.float32),
        lax.psum_scatter(
            grad_key_w.astype(jnp.bfloat16), "dp", scatter_dimension=0, tiled=True
        ).astype(jnp.float32),
        lax.psum_scatter(
            grad_value_w.astype(jnp.bfloat16), "dp", scatter_dimension=0, tiled=True
        ).astype(jnp.float32),
        lax.psum_scatter(
            grad_output_w.astype(jnp.bfloat16), "dp", scatter_dimension=0, tiled=True
        ).astype(jnp.float32),
    )
    grad_gate, grad_up, grad_down = (
        lax.psum_scatter(
            grad_gate_w.astype(jnp.bfloat16), "dp", scatter_dimension=0, tiled=True
        ).astype(jnp.float32),
        lax.psum_scatter(
            grad_up_w.astype(jnp.bfloat16), "dp", scatter_dimension=0, tiled=True
        ).astype(jnp.float32),
        lax.psum_scatter(
            grad_down_w.astype(jnp.bfloat16), "dp", scatter_dimension=0, tiled=True
        ).astype(jnp.float32),
    )
    attn_gain_sum, mlp_gain_sum = (
        lax.psum_scatter(grad_attn_gain, ("dp", "tensor"), scatter_dimension=0, tiled=True),
        lax.psum_scatter(grad_mlp_gain, ("dp", "tensor"), scatter_dimension=0, tiled=True),
    )
    return (
        block_out,
        grad_tokens,
        grad_query,
        grad_key,
        grad_value,
        grad_output,
        attn_gain_sum,
        grad_gate,
        grad_up,
        grad_down,
        mlp_gain_sum,
    )


PAIR = 2 * HEAD


def lane_tables():
    half = HEAD // 2
    lanes = jnp.arange(PAIR)
    freqs = rope_base ** (-2.0 * (lanes % half).astype(jnp.float32) / HEAD)
    angles = jnp.arange(LEN).astype(jnp.float32)[:, None] * freqs[None, :]
    signs = jnp.where(lanes % HEAD < half, -1.0, 1.0)
    return (jnp.cos(angles), jnp.sin(angles) * signs[None, :])


def swap_halves(values, lanes):
    half = HEAD // 2
    return jnp.where(
        lanes % HEAD < half,
        pltpu.roll(values, PAIR - half, 1),
        pltpu.roll(values, half, 1),
    )


def dot_last(left, right):
    return lax.dot_general(
        left, right, (((1,), (1,)), ((), ())), preferred_element_type=jnp.float32
    )


def dot_first(left, right):
    return lax.dot_general(
        left, right, (((0,), (0,)), ((), ())), preferred_element_type=jnp.float32
    )


def forward_kernel(q_ref, k_ref, v_ref, cos_ref, sin_ref, qr_ref, kr_ref, vb_ref, mix_ref):
    lanes = lax.broadcasted_iota(jnp.int32, (LEN, PAIR), 1)
    cosine = cos_ref[...]
    sine = sin_ref[...]

    def rotated(values):
        return (values * cosine + swap_halves(values, lanes) * sine).astype(jnp.bfloat16)

    query = rotated(q_ref[...])
    key = rotated(k_ref[...])
    value = v_ref[...].astype(jnp.bfloat16)
    qr_ref[...] = query
    kr_ref[...] = key
    vb_ref[...] = value
    scaled = query * jnp.bfloat16(HEAD**-0.5)
    step = LEN // 2
    for part in range(2):
        rows = slice(part * step, (part + 1) * step)
        seen = (part + 1) * step
        shape = (step, seen)
        allowed = lax.broadcasted_iota(jnp.int32, shape, 0) + part * step >= (
            lax.broadcasted_iota(jnp.int32, shape, 1)
        )
        mixed = []
        for head in range(2):
            mine = lanes[rows] // HEAD == head
            one_head = jnp.where(mine, scaled[rows], jnp.zeros_like(scaled[rows]))
            scores = jnp.where(allowed, dot_last(one_head, key[:seen]), -1e30)
            top = jnp.max(scores, axis=-1, keepdims=True)
            expo = jnp.exp(scores - top)
            total = jnp.sum(expo, axis=-1, keepdims=True)
            probs = (expo * (1.0 / total)).astype(jnp.bfloat16)
            mixed.append(jnp.dot(probs, value[:seen], preferred_element_type=jnp.float32))
        both = jnp.where(lanes[rows] < HEAD, mixed[0], mixed[1])
        mix_ref[rows, :] = both.astype(jnp.bfloat16)


def backward_kernel(q_ref, k_ref, v_ref, g_ref, cos_ref, sin_ref, out_ref):
    lanes = lax.broadcasted_iota(jnp.int32, (LEN, PAIR), 1)
    cosine = cos_ref[...]
    sine = sin_ref[...]
    factor = jnp.bfloat16(HEAD**-0.5)
    query = q_ref[...] * factor
    key = k_ref[...]
    key_scaled = key * factor
    value = v_ref[...]
    grad = g_ref[...]
    step = LEN // 2
    grad_query, grad_key, grad_value = [], [], []
    for part in range(2):
        rows = slice(part * step, (part + 1) * step)
        seen = (part + 1) * step
        shape = (seen, step)
        allowed = lax.broadcasted_iota(jnp.int32, shape, 1) + part * step >= (
            lax.broadcasted_iota(jnp.int32, shape, 0)
        )
        for head in range(2):
            mine = lanes[rows] // HEAD == head
            own = lanes[:seen] // HEAD == head
            q_one = jnp.where(mine, query[rows], jnp.zeros_like(query[rows]))
            g_one = jnp.where(mine, grad[rows], jnp.zeros_like(grad[rows]))
            k_one = jnp.where(own, key_scaled[:seen], jnp.zeros_like(key[:seen]))
            scores = jnp.where(allowed, dot_last(key[:seen], q_one), -1e30)
            top = jnp.max(scores, axis=0, keepdims=True)
            expo = jnp.exp(scores - top)
            total = jnp.sum(expo, axis=0, keepdims=True)
            probs = expo * (1.0 / total)
            grad_probs = dot_last(value[:seen], g_one)
            inner = jnp.sum(probs * grad_probs, axis=0, keepdims=True)
            grad_scores = (probs * (grad_probs - inner)).astype(jnp.bfloat16)
            rounded = probs.astype(jnp.bfloat16)
            grad_value.append(jnp.dot(rounded, g_one, preferred_element_type=jnp.float32))
            grad_key.append(jnp.dot(grad_scores, q_one, preferred_element_type=jnp.float32))
            grad_query.append(dot_first(grad_scores, k_one))

    def gather(parts):
        first = parts[0] + parts[1]
        second = parts[2] + parts[3]
        return jnp.concatenate([first + second[:step], second[step:]], axis=0)

    def unrotated(values):
        return (values * cosine - swap_halves(values, lanes) * sine).astype(jnp.bfloat16)

    all_query = jnp.concatenate(
        [grad_query[0] + grad_query[1], grad_query[2] + grad_query[3]], axis=0
    )
    columns = out_ref.shape[1] // 3
    place = pl.multiple_of(pl.program_id(0) * PAIR, PAIR)
    out_ref[:, pl.ds(place, PAIR)] = unrotated(all_query)
    out_ref[:, pl.ds(columns + place, PAIR)] = unrotated(gather(grad_key))
    out_ref[:, pl.ds(2 * columns + place, PAIR)] = gather(grad_value).astype(jnp.bfloat16)


def pair_block(offset):
    return pl.BlockSpec((LEN, PAIR), lambda step: (0, offset + step))


def whole_block(columns):
    return pl.BlockSpec((LEN, columns), lambda step: (0, 0))


def attention(qkv, cosine, sine):
    columns = qkv.shape[1] // 3
    pairs = columns // PAIR
    flat = jax.ShapeDtypeStruct((LEN, columns), jnp.bfloat16)
    return pl.pallas_call(
        forward_kernel,
        grid=(pairs,),
        in_specs=[pair_block(0), pair_block(pairs), pair_block(2 * pairs)]
        + [whole_block(PAIR)] * 2,
        out_specs=[pair_block(0)] * 4,
        out_shape=[flat] * 4,
        name="attend",
        cost_estimate=pl.CostEstimate(
            flops=8 * LEN * LEN * columns,
            transcendentals=LEN * LEN * columns // HEAD,
            bytes_accessed=20 * LEN * columns,
        ),
    )(qkv, qkv, qkv, cosine, sine)


def attention_back(query, key, value, grad, cosine, sine):
    columns = query.shape[1]
    return pl.pallas_call(
        backward_kernel,
        grid=(columns // PAIR,),
        in_specs=[pair_block(0)] * 4 + [whole_block(PAIR)] * 2,
        out_specs=whole_block(3 * columns),
        out_shape=jax.ShapeDtypeStruct((LEN, 3 * columns), jnp.bfloat16),
        name="attend_back",
        cost_estimate=pl.CostEstimate(
            flops=20 * LEN * LEN * columns,
            transcendentals=LEN * LEN * columns // HEAD,
            bytes_accessed=14 * LEN * columns,
        ),
    )(query, key, value, grad, cosine, sine)


TILE = 256


def unit_kernel(norm_ref, grad_ref, gate_ref, up_ref, down_ref, activ_ref, pre_ref):
    rows = norm_ref[...]
    gate = jnp.dot(rows, gate_ref[...], preferred_element_type=jnp.float32)
    up = jnp.dot(rows, up_ref[...], preferred_element_type=jnp.float32)
    grad_activ = jnp.dot(grad_ref[...], down_ref[...], preferred_element_type=jnp.float32)
    sigma = jax.nn.sigmoid(gate)
    swish = gate * sigma
    activ_ref[...] = (swish * up).astype(jnp.bfloat16)
    grad_gate = grad_activ * up * sigma * (1.0 + gate * (1.0 - sigma))
    place = pl.multiple_of(pl.program_id(0) * TILE, TILE)
    units = pre_ref.shape[1] // 2
    pre_ref[:, pl.ds(place, TILE)] = grad_gate.astype(jnp.bfloat16)
    pre_ref[:, pl.ds(units + place, TILE)] = (grad_activ * swish).astype(jnp.bfloat16)


def hidden_units_pass(normed, grads, gate_up, down):
    rows, width = normed.shape
    units = down.shape[1]
    steps = units // TILE
    whole = pl.BlockSpec((rows, width), lambda step: (0, 0))

    def tile(offset):
        return pl.BlockSpec((width, TILE), lambda step: (0, offset + step))

    return pl.pallas_call(
        unit_kernel,
        grid=(steps,),
        in_specs=[whole, whole, tile(0), tile(steps), tile(0)],
        out_specs=[
            pl.BlockSpec((rows, TILE), lambda step: (0, step)),
            pl.BlockSpec((rows, 2 * units), lambda step: (0, 0)),
        ],
        out_shape=[
            jax.ShapeDtypeStruct((rows, units), jnp.bfloat16),
            jax.ShapeDtypeStruct((rows, 2 * units), jnp.bfloat16),
        ],
        name="units",
        cost_estimate=pl.CostEstimate(
            flops=rows * width * units, transcendentals=0, bytes_accessed=4 * rows * width
        ),
    )(normed, grads, gate_up, gate_up, down)


def rows_kernel(left_ref, right_ref, out_ref):
    out_ref[...] = dot_last(left_ref[...], right_ref[...]).astype(out_ref.dtype)


def times_rows(left, right, dtype):
    rows, depth = left.shape
    width = right.shape[0]
    return pl.pallas_call(
        rows_kernel,
        grid=(width // TILE,),
        in_specs=[
            pl.BlockSpec((rows, depth), lambda step: (0, 0)),
            pl.BlockSpec((TILE, depth), lambda step: (step, 0)),
        ],
        out_specs=pl.BlockSpec((rows, TILE), lambda step: (0, step)),
        out_shape=jax.ShapeDtypeStruct((rows, width), dtype),
        name="sums",
        cost_estimate=pl.CostEstimate(
            flops=rows * width * depth // 4, transcendentals=0, bytes_accessed=rows * width
        ),
    )(left, right)


def shift(values, count):
    return lax.ppermute(values, "tensor", [(i, (i + 1) % count) for i in range(count)])


def after(values, *earlier):
    return lax.optimization_barrier((values,) + earlier)[0]


PEERS = 8
ORDER = (0, 2, 4, 6, 1, 3, 5, 7)


def peer(values, hop):
    return lax.ppermute(values, "dp", [(i, i ^ hop) for i in range(PEERS)])


def by_peer(values):
    width = values.shape[1] // PEERS
    blocks = [values[:, k * width : (k + 1) * width] for k in range(PEERS)]
    me = lax.axis_index("dp")
    for hop in (1, 2, 4):
        blocks = [jnp.where(me & hop, blocks[k ^ hop], blocks[k]) for k in range(PEERS)]
    half = PEERS // 2
    near = jnp.concatenate([blocks[k] for k in ORDER[:half]], axis=1)
    far = jnp.concatenate([blocks[k] for k in ORDER[half:]], axis=1)
    return near, far


def corner_step(kept):
    rows = kept.shape[0] // 4
    half = rows // 2
    mine, over_x, over_y, corner = [kept[k * rows : (k + 1) * rows] for k in range(4)]
    from_y, from_x = peer(corner[:half], 4), peer(corner[half:], 2)
    over_x = jnp.concatenate([over_x[:half] + from_y, over_x[half:]], axis=0)
    over_y = jnp.concatenate([over_y[:half], over_y[half:] + from_x], axis=0)
    return mine, over_x, over_y


def cross_step(mine, over_x, over_y):
    over_x, over_y = peer(over_x, 2), peer(over_y, 4)
    return mine.astype(jnp.float32) + over_x.astype(jnp.float32) + over_y.astype(jnp.float32)


def travel(values, count):
    stops = [values]
    for _ in range(count - 1):
        stops.append(shift(stops[-1], count))
    return stops


def ring_sum(parts, count):
    total = parts[1]
    for j in list(range(2, count)) + [0]:
        total = shift(total.astype(jnp.bfloat16), count).astype(jnp.float32) + parts[j]
    return total


def sum_all(values, axes):
    for name, count in axes:
        hop = 1
        while hop < count:
            values = values + lax.ppermute(values, name, [(i, i ^ hop) for i in range(count)])
            hop *= 2
    return values


def token_parallel(
    tokens, w_query, w_key, w_value, w_output, attn_gain, w_gate, w_up, w_down, mlp_gain, cotangent
):
    count = lax.axis_size("tensor")
    dp_count = lax.axis_size("dp")
    heads = w_query.shape[1]
    hidden_units = w_gate.shape[1]
    gains = lax.all_gather(jnp.stack([attn_gain, mlp_gain]), "dp", axis=0)
    gains = jnp.swapaxes(gains, 0, 1).reshape(2, -1).astype(jnp.float32)
    attn_scale, mlp_scale = gains[0], gains[1]
    shard = jnp.concatenate([w_query, w_key, w_value, w_output], axis=1)
    own = lax.all_gather(shard, "dp", axis=0, tiled=True)
    others = travel(shard, count)[1:]
    rest_shard = jnp.concatenate(
        [other[:, k * heads : (k + 1) * heads] for k in range(4) for other in others], axis=1
    )
    rest = lax.all_gather(rest_shard, "dp", axis=0, tiled=True)
    wide = (count - 1) * heads
    gate_up_shard = after(jnp.concatenate([w_gate, w_up], axis=1), rest_shard)
    gate_up = lax.all_gather(gate_up_shard, "dp", axis=0, tiled=True)
    down = lax.all_gather(after(w_down, rest_shard), "dp", axis=0, tiled=True)

    source = tokens.astype(jnp.float32)
    inverse_one = lax.rsqrt(jnp.mean(source * source, axis=-1, keepdims=True) + eps)
    normed_one = (source * inverse_one * attn_scale).astype(jnp.bfloat16)
    near_one, far_one = by_peer(normed_one)
    cosine, sine = lane_tables()
    own_qkv = jnp.dot(normed_one, own[:, : 3 * heads], preferred_element_type=jnp.float32)
    own_query, own_key, own_value, own_mixed = attention(own_qkv, cosine, sine)
    cotangents = [cotangent, shift(after(cotangent, others[-1]), count)]
    for _ in range(count - 2):
        cotangents.append(shift(after(cotangents[-1], own_mixed), count))
    rest = after(rest, *cotangents[:-1])
    rest_qkv = jnp.dot(normed_one, rest[:, : 3 * wide], preferred_element_type=jnp.float32)
    rest_query, rest_key, rest_value, rest_mixed = attention(rest_qkv, cosine, sine)
    branch = contract_cols(own_mixed, own[:, 3 * heads :])
    branch = branch + contract_cols(rest_mixed, rest[:, 3 * wide :])
    hidden = source + after(branch, cotangents[-1])
    inverse_two = lax.rsqrt(jnp.mean(hidden * hidden, axis=-1, keepdims=True) + eps)
    normed_two = (hidden * inverse_two * mlp_scale).astype(jnp.bfloat16)

    normed = travel(normed_two, count)
    activs, pres, norm_parts = [], [], []
    arrived = None
    for j in range(count):
        earlier = (normed[2],) if j == 1 else (norm_total,) if j == 3 else ()
        rows = after(normed[j], *earlier)
        activ, pre = hidden_units_pass(rows, cotangents[j], gate_up, down)
        norm_part = times_rows(pre, gate_up, jnp.float32)
        if j == 1:
            norm_total = norm_part.astype(jnp.bfloat16)
        elif j > 1:
            arrived = shift(norm_total, count)
            norm_total = (arrived.astype(jnp.float32) + norm_part).astype(jnp.bfloat16)
        activs.append(activ)
        pres.append(pre)
        norm_parts.append(norm_part)
    arrived = shift(norm_total, count)
    all_normed = jnp.concatenate(normed, axis=0)
    all_cotangents = jnp.concatenate(cotangents, axis=0)
    activs[-1] = after(activs[-1], norm_total)
    grad_down_w = contract_rows(all_cotangents, jnp.concatenate(activs, axis=0)).astype(
        jnp.bfloat16
    )
    pres[-1] = after(pres[-1], grad_down_w, norm_total)
    grad_gate_up_w = contract_rows(all_normed, jnp.concatenate(pres, axis=0)).astype(jnp.bfloat16)
    grad_normed_two = arrived.astype(jnp.float32) + after(
        norm_parts[0], grad_gate_up_w, grad_down_w
    )

    def over_dp(values):
        return lax.psum_scatter(values, "dp", scatter_dimension=0, tiled=True)

    grad_gate_up = over_dp(grad_gate_up_w).astype(jnp.float32)
    grad_down = over_dp(grad_down_w).astype(jnp.float32)

    grad_hidden_norm, mlp_gain_part = norm_back(grad_normed_two, hidden, inverse_two, mlp_scale)
    grad_hidden = cotangent.astype(jnp.float32) + grad_hidden_norm
    grad_branch = grad_hidden.astype(jnp.bfloat16)
    all_mixed = jnp.concatenate([own_mixed, rest_mixed], axis=1)
    near_branch, far_branch = by_peer(grad_branch)
    output_far = contract_rows(far_branch, all_mixed).astype(jnp.bfloat16)
    rest_grad = jnp.dot(
        after(grad_branch, output_far), rest[:, 3 * wide :], preferred_element_type=jnp.float32
    ).astype(jnp.bfloat16)
    output_near = contract_rows(near_branch, after(all_mixed, rest_grad))
    output_near = (output_near + peer(output_far, 1).astype(jnp.float32)).astype(jnp.bfloat16)
    output_parts = corner_step(output_near)
    rest_grad = after(rest_grad, output_near, grad_down)
    rest_pre = attention_back(rest_query, rest_key, rest_value, rest_grad, cosine, sine)

    def mlp_part(j, stage):
        return times_rows(after(activs[j], stage), down, jnp.bfloat16)

    mlp_arrived = shift(mlp_part(1, grad_branch), count)
    mlp_next = mlp_part(2, output_far)
    rest_pre = after(rest_pre, mlp_arrived, *output_parts)
    mlp_total = (mlp_arrived.astype(jnp.float32) + after(mlp_next, rest_pre)).astype(jnp.bfloat16)
    mlp_arrived = shift(mlp_total, count)
    rest_far = contract_rows(far_one, rest_pre).astype(jnp.bfloat16)
    output_sum = cross_step(*output_parts)
    rest_later = after(rest_pre, rest_far)
    grad_normed_one = contract_cols(rest_later, rest[:, : 3 * wide])
    rest_later = after(rest_later, grad_normed_one, output_sum)
    rest_near = contract_rows(near_one, rest_later) + peer(rest_far, 1).astype(jnp.float32)
    rest_near = rest_near.astype(jnp.bfloat16)
    rest_parts = corner_step(rest_near)
    own_grad = jnp.dot(
        after(grad_branch, rest_near), own[:, 3 * heads :], preferred_element_type=jnp.float32
    ).astype(jnp.bfloat16)
    own_pre = attention_back(own_query, own_key, own_value, own_grad, cosine, sine)
    own_pre = after(own_pre, mlp_arrived, grad_gate_up, *rest_parts)
    mlp_next = after(mlp_part(3, rest_far), own_pre)
    mlp_total = (mlp_arrived.astype(jnp.float32) + mlp_next).astype(jnp.bfloat16)
    mlp_total = shift(mlp_total, count).astype(jnp.float32) + mlp_part(0, rest_near)
    rest_sum = cross_step(*rest_parts)
    own_far = contract_rows(far_one, own_pre).astype(jnp.bfloat16)
    own_later = after(own_pre, own_far)
    grad_normed_one = grad_normed_one + contract_cols(own_later, own[:, : 3 * heads])
    own_near = contract_rows(near_one, own_later) + peer(own_far, 1).astype(jnp.float32)
    own_sum = cross_step(*corner_step(own_near.astype(jnp.bfloat16)))
    block_out = (hidden + mlp_total).astype(jnp.bfloat16)

    grad_source_norm, attn_gain_part = norm_back(grad_normed_one, source, inverse_one, attn_scale)
    grad_tokens = (grad_hidden + grad_source_norm).astype(jnp.bfloat16)

    def group_slot(j):
        if not j:
            return own_sum
        columns = [rest_sum[:, k * wide + (j - 1) * heads : k * wide + j * heads] for k in range(3)]
        return jnp.concatenate(columns, axis=1)

    qkv = ring_sum([group_slot(j) for j in range(count)], count)
    grad_query, grad_key, grad_value = [qkv[:, k * heads : (k + 1) * heads] for k in range(3)]
    grad_output = ring_sum(
        [output_sum[:, j * heads : (j + 1) * heads].astype(jnp.float32) for j in range(count)], count
    )
    gain_parts = sum_all(
        jnp.stack([attn_gain_part, mlp_gain_part]), (("dp", dp_count), ("tensor", count))
    )
    piece = gain_parts.shape[1] // (dp_count * count)
    place = (lax.axis_index("dp") * count + lax.axis_index("tensor")) * piece
    gain_sums = lax.dynamic_slice_in_dim(gain_parts, place, piece, axis=1)
    return (
        block_out,
        grad_tokens,
        grad_query,
        grad_key,
        grad_value,
        grad_output,
        gain_sums[0],
        grad_gate_up[:, :hidden_units],
        grad_gate_up[:, hidden_units:],
        grad_down,
        gain_sums[1],
    )


def local(tokens, w_query, *others):
    axes = (lax.axis_size("dp"), lax.axis_size("tensor"))
    whole = tokens.shape[0] == LEN and w_query.shape[1] % PAIR == 0
    if whole and axes[0] == PEERS and axes[1] == 4:
        return token_parallel(tokens, w_query, *others)
    return tensor_parallel(tokens, w_query, *others)


def solution(mesh):
    in_specs = (
        P(("dp", "tensor"), None),
        P("dp", "tensor"),
        P("dp", "tensor"),
        P("dp", "tensor"),
        P("dp", "tensor"),
        P("dp"),
        P("dp", "tensor"),
        P("dp", "tensor"),
        P("dp", "tensor"),
        P("dp"),
        P(("dp", "tensor"), None),
    )
    out_specs = (
        P(("dp", "tensor"), None),
        P(("dp", "tensor"), None),
        P("dp", "tensor"),
        P("dp", "tensor"),
        P("dp", "tensor"),
        P("dp", "tensor"),
        P(("dp", "tensor")),
        P("dp", "tensor"),
        P("dp", "tensor"),
        P("dp", "tensor"),
        P(("dp", "tensor")),
    )
    return jax.shard_map(local, mesh=mesh, in_specs=in_specs, out_specs=out_specs, check_vma=False)
```

```python
import jax
import jax.numpy as jnp
from jax import lax
from jax.experimental import pallas as pl
from jax.experimental.pallas import tpu as pltpu
from jax.sharding import PartitionSpec as P

HEAD = 64
LEN = 512


eps = 1e-05
rope_base = 130000.0


def tables(rows):
    half = HEAD // 2
    places = (jnp.arange(rows) % LEN).astype(jnp.float32)
    freqs = rope_base ** (-2.0 * jnp.arange(half).astype(jnp.float32) / HEAD)
    angles = places[:, None] * freqs[None, :]
    return (jnp.cos(angles)[:, None, :], jnp.sin(angles)[:, None, :])


def rotate(values, cosine, sine):
    half = values.shape[-1] // 2
    first = values[..., :half]
    second = values[..., half:]
    return jnp.concatenate(
        [first * cosine - second * sine, second * cosine + first * sine], axis=-1
    )


def contract_rows(left, right):
    return lax.dot_general(
        left, right, (((0,), (0,)), ((), ())), preferred_element_type=jnp.float32
    )


def contract_cols(left, right):
    return lax.dot_general(
        left, right, (((1,), (1,)), ((), ())), preferred_element_type=jnp.float32
    )


def causal_scores(query_seq, key_seq):
    scores = jnp.einsum("qhd,khd->hqk", query_seq, key_seq, preferred_element_type=jnp.float32)
    scores = scores * HEAD ** (-0.5)
    length = query_seq.shape[0]
    allowed = jnp.arange(length)[:, None] >= jnp.arange(length)[None, :]
    return jnp.where(allowed[None], scores, -1e30)


def attend_forward(block):
    query_seq, key_seq, value_seq = block
    scores = causal_scores(query_seq, key_seq)
    top = jnp.max(scores, axis=-1, keepdims=True)
    expo = jnp.exp(scores - top)
    total = jnp.sum(expo, axis=-1, keepdims=True)
    probs = (expo / total).astype(jnp.bfloat16)
    attended = jnp.einsum("hqk,khd->qhd", probs, value_seq, preferred_element_type=jnp.float32)
    return (attended, top + jnp.log(total))


def attend_backward(block):
    query_seq, key_seq, value_seq, log_total, grad_seq = block
    scores = causal_scores(query_seq, key_seq)
    probs = jnp.exp(scores - log_total)
    grad_probs = jnp.einsum("qhd,khd->hqk", grad_seq, value_seq, preferred_element_type=jnp.float32)
    inner = jnp.sum(probs * grad_probs, axis=-1, keepdims=True)
    grad_scores = (probs * (grad_probs - inner)).astype(jnp.bfloat16)
    factor = HEAD ** (-0.5)
    grad_query = (
        jnp.einsum("hqk,khd->qhd", grad_scores, key_seq, preferred_element_type=jnp.float32)
        * factor
    )
    grad_key = (
        jnp.einsum("hqk,qhd->khd", grad_scores, query_seq, preferred_element_type=jnp.float32)
        * factor
    )
    grad_value = jnp.einsum(
        "hqk,qhd->khd", probs.astype(jnp.bfloat16), grad_seq, preferred_element_type=jnp.float32
    )
    return (grad_query, grad_key, grad_value)


def norm_back(grad_normed, source, inverse, gain):
    scaled = grad_normed * gain
    inner = jnp.mean(scaled * source, axis=-1, keepdims=True)
    grad_source = inverse * scaled - source * inverse**3 * inner
    grad_gain = jnp.sum(grad_normed * source * inverse, axis=0)
    return (grad_source, grad_gain)


def tensor_parallel(
    tokens, w_query, w_key, w_value, w_output, attn_gain, w_gate, w_up, w_down, mlp_gain, cotangent
):
    query_full, key_full, value_full, output_full, attn_scale = (
        lax.all_gather(w_query, "dp", axis=0, tiled=True),
        lax.all_gather(w_key, "dp", axis=0, tiled=True),
        lax.all_gather(w_value, "dp", axis=0, tiled=True),
        lax.all_gather(w_output, "dp", axis=0, tiled=True),
        lax.all_gather(attn_gain, "dp", axis=0, tiled=True),
    )
    gate_full, up_full, down_full, mlp_scale = (
        lax.all_gather(w_gate, "dp", axis=0, tiled=True),
        lax.all_gather(w_up, "dp", axis=0, tiled=True),
        lax.all_gather(w_down, "dp", axis=0, tiled=True),
        lax.all_gather(mlp_gain, "dp", axis=0, tiled=True),
    )
    attn_scale = attn_scale.astype(jnp.float32)
    mlp_scale = mlp_scale.astype(jnp.float32)
    source = tokens.astype(jnp.float32)
    inverse_one = lax.rsqrt(jnp.mean(source * source, axis=-1, keepdims=True) + eps)
    normed_one = (source * inverse_one * attn_scale).astype(jnp.bfloat16)
    gathered_one = lax.all_gather(normed_one, "tensor", axis=0, tiled=True)
    rows = gathered_one.shape[0]
    local_heads = query_full.shape[1] // HEAD
    seq_count = rows // LEN
    cosine, sine = tables(rows)

    def by_seq(values):
        return values.reshape(seq_count, LEN, local_heads, HEAD)

    queries = jnp.dot(gathered_one, query_full, preferred_element_type=jnp.float32).reshape(
        rows, local_heads, HEAD
    )
    keys = jnp.dot(gathered_one, key_full, preferred_element_type=jnp.float32).reshape(
        rows, local_heads, HEAD
    )
    values = jnp.dot(gathered_one, value_full, preferred_element_type=jnp.float32).astype(
        jnp.bfloat16
    )
    query_rot = rotate(queries, cosine, sine).astype(jnp.bfloat16)
    key_rot = rotate(keys, cosine, sine).astype(jnp.bfloat16)
    attended, log_total = lax.map(
        attend_forward, (by_seq(query_rot), by_seq(key_rot), by_seq(values))
    )
    mixed_heads = attended.reshape(rows, local_heads * HEAD).astype(jnp.bfloat16)
    part = mixed_heads
    attn_branch = lax.psum_scatter(
        contract_cols(part, output_full), "tensor", scatter_dimension=0, tiled=True
    )
    hidden = source + attn_branch
    inverse_two = lax.rsqrt(jnp.mean(hidden * hidden, axis=-1, keepdims=True) + eps)
    normed_two = (hidden * inverse_two * mlp_scale).astype(jnp.bfloat16)
    gathered_two = lax.all_gather(normed_two, "tensor", axis=0, tiled=True)
    gate = jnp.dot(gathered_two, gate_full, preferred_element_type=jnp.float32)
    up = jnp.dot(gathered_two, up_full, preferred_element_type=jnp.float32)
    sigma = jax.nn.sigmoid(gate)
    swish = gate * sigma
    activ = (swish * up).astype(jnp.bfloat16)
    part = activ
    mlp_branch = lax.psum_scatter(
        contract_cols(part, down_full).astype(jnp.bfloat16),
        "tensor",
        scatter_dimension=0,
        tiled=True,
    ).astype(jnp.float32)
    block_out = (hidden + mlp_branch).astype(jnp.bfloat16)
    gate_back, up_back, down_back = (
        lax.all_gather(w_gate, "dp", axis=0, tiled=True),
        lax.all_gather(w_up, "dp", axis=0, tiled=True),
        lax.all_gather(w_down, "dp", axis=0, tiled=True),
    )
    grad_out_rows = lax.all_gather(cotangent, "tensor", axis=0, tiled=True)
    grad_activ = jnp.dot(grad_out_rows, down_back, preferred_element_type=jnp.float32)
    grad_gate_pre = (grad_activ * up * sigma * (1.0 + gate * (1.0 - sigma))).astype(jnp.bfloat16)
    grad_up_pre = (grad_activ * swish).astype(jnp.bfloat16)
    grad_down_w = contract_rows(grad_out_rows, activ)
    grad_gate_w = contract_rows(gathered_two, grad_gate_pre)
    grad_up_w = contract_rows(gathered_two, grad_up_pre)
    grad_normed_two = lax.psum_scatter(
        contract_cols(grad_gate_pre, gate_back) + contract_cols(grad_up_pre, up_back),
        "tensor",
        scatter_dimension=0,
        tiled=True,
    )
    grad_hidden_norm, grad_mlp_gain = norm_back(grad_normed_two, hidden, inverse_two, mlp_scale)
    grad_hidden = cotangent.astype(jnp.float32) + grad_hidden_norm
    grad_branch = grad_hidden.astype(jnp.bfloat16)
    grad_branch_rows = lax.all_gather(grad_branch, "tensor", axis=0, tiled=True)
    grad_mixed = jnp.dot(grad_branch_rows, output_full, preferred_element_type=jnp.float32).astype(
        jnp.bfloat16
    )
    grad_output_w = contract_rows(grad_branch_rows, mixed_heads)
    grad_query_rot, grad_key_rot, grad_value_seq = lax.map(
        attend_backward,
        (by_seq(query_rot), by_seq(key_rot), by_seq(values), log_total, by_seq(grad_mixed)),
    )
    grad_q_pre = rotate(grad_query_rot.reshape(rows, local_heads, HEAD), cosine, -sine)
    grad_q_pre = grad_q_pre.reshape(rows, local_heads * HEAD).astype(jnp.bfloat16)
    grad_k_pre = rotate(grad_key_rot.reshape(rows, local_heads, HEAD), cosine, -sine)
    grad_k_pre = grad_k_pre.reshape(rows, local_heads * HEAD).astype(jnp.bfloat16)
    grad_v_pre = grad_value_seq.reshape(rows, local_heads * HEAD).astype(jnp.bfloat16)
    grad_query_w = contract_rows(gathered_one, grad_q_pre)
    grad_key_w = contract_rows(gathered_one, grad_k_pre)
    grad_value_w = contract_rows(gathered_one, grad_v_pre)
    total = contract_cols(grad_q_pre, query_full) + contract_cols(grad_k_pre, key_full)
    grad_normed_one = lax.psum_scatter(
        (total + contract_cols(grad_v_pre, value_full)).astype(jnp.bfloat16),
        "tensor",
        scatter_dimension=0,
        tiled=True,
    ).astype(jnp.float32)
    grad_source_norm, grad_attn_gain = norm_back(grad_normed_one, source, inverse_one, attn_scale)
    grad_tokens = (grad_hidden + grad_source_norm).astype(jnp.bfloat16)
    grad_query, grad_key, grad_value, grad_output = (
        lax.psum_scatter(
            grad_query_w.astype(jnp.bfloat16), "dp", scatter_dimension=0, tiled=True
        ).astype(jnp.float32),
        lax.psum_scatter(
            grad_key_w.astype(jnp.bfloat16), "dp", scatter_dimension=0, tiled=True
        ).astype(jnp.float32),
        lax.psum_scatter(
            grad_value_w.astype(jnp.bfloat16), "dp", scatter_dimension=0, tiled=True
        ).astype(jnp.float32),
        lax.psum_scatter(
            grad_output_w.astype(jnp.bfloat16), "dp", scatter_dimension=0, tiled=True
        ).astype(jnp.float32),
    )
    grad_gate, grad_up, grad_down = (
        lax.psum_scatter(
            grad_gate_w.astype(jnp.bfloat16), "dp", scatter_dimension=0, tiled=True
        ).astype(jnp.float32),
        lax.psum_scatter(
            grad_up_w.astype(jnp.bfloat16), "dp", scatter_dimension=0, tiled=True
        ).astype(jnp.float32),
        lax.psum_scatter(
            grad_down_w.astype(jnp.bfloat16), "dp", scatter_dimension=0, tiled=True
        ).astype(jnp.float32),
    )
    attn_gain_sum, mlp_gain_sum = (
        lax.psum_scatter(grad_attn_gain, ("dp", "tensor"), scatter_dimension=0, tiled=True),
        lax.psum_scatter(grad_mlp_gain, ("dp", "tensor"), scatter_dimension=0, tiled=True),
    )
    return (
        block_out,
        grad_tokens,
        grad_query,
        grad_key,
        grad_value,
        grad_output,
        attn_gain_sum,
        grad_gate,
        grad_up,
        grad_down,
        mlp_gain_sum,
    )


PAIR = 2 * HEAD


def lane_tables():
    half = HEAD // 2
    lanes = jnp.arange(PAIR)
    freqs = rope_base ** (-2.0 * (lanes % half).astype(jnp.float32) / HEAD)
    angles = jnp.arange(LEN).astype(jnp.float32)[:, None] * freqs[None, :]
    signs = jnp.where(lanes % HEAD < half, -1.0, 1.0)
    return (jnp.cos(angles), jnp.sin(angles) * signs[None, :])


def swap_halves(values, lanes):
    half = HEAD // 2
    return jnp.where(
        lanes % HEAD < half,
        pltpu.roll(values, PAIR - half, 1),
        pltpu.roll(values, half, 1),
    )


def dot_last(left, right):
    return lax.dot_general(
        left, right, (((1,), (1,)), ((), ())), preferred_element_type=jnp.float32
    )


def dot_first(left, right):
    return lax.dot_general(
        left, right, (((0,), (0,)), ((), ())), preferred_element_type=jnp.float32
    )


def forward_kernel(q_ref, k_ref, v_ref, cos_ref, sin_ref, qr_ref, kr_ref, vb_ref, mix_ref):
    lanes = lax.broadcasted_iota(jnp.int32, (LEN, PAIR), 1)
    cosine = cos_ref[...]
    sine = sin_ref[...]

    def rotated(values):
        return (values * cosine + swap_halves(values, lanes) * sine).astype(jnp.bfloat16)

    query = rotated(q_ref[...])
    key = rotated(k_ref[...])
    value = v_ref[...].astype(jnp.bfloat16)
    qr_ref[...] = query
    kr_ref[...] = key
    vb_ref[...] = value
    scaled = query * jnp.bfloat16(HEAD**-0.5)
    step = LEN // 2
    for part in range(2):
        rows = slice(part * step, (part + 1) * step)
        seen = (part + 1) * step
        shape = (step, seen)
        allowed = lax.broadcasted_iota(jnp.int32, shape, 0) + part * step >= (
            lax.broadcasted_iota(jnp.int32, shape, 1)
        )
        mixed = []
        for head in range(2):
            mine = lanes[rows] // HEAD == head
            one_head = jnp.where(mine, scaled[rows], jnp.zeros_like(scaled[rows]))
            scores = jnp.where(allowed, dot_last(one_head, key[:seen]), -1e30)
            top = jnp.max(scores, axis=-1, keepdims=True)
            expo = jnp.exp(scores - top)
            total = jnp.sum(expo, axis=-1, keepdims=True)
            probs = (expo * (1.0 / total)).astype(jnp.bfloat16)
            mixed.append(jnp.dot(probs, value[:seen], preferred_element_type=jnp.float32))
        both = jnp.where(lanes[rows] < HEAD, mixed[0], mixed[1])
        mix_ref[rows, :] = both.astype(jnp.bfloat16)


def backward_kernel(q_ref, k_ref, v_ref, g_ref, cos_ref, sin_ref, out_ref):
    lanes = lax.broadcasted_iota(jnp.int32, (LEN, PAIR), 1)
    cosine = cos_ref[...]
    sine = sin_ref[...]
    factor = jnp.bfloat16(HEAD**-0.5)
    query = q_ref[...] * factor
    key = k_ref[...]
    key_scaled = key * factor
    value = v_ref[...]
    grad = g_ref[...]
    step = LEN // 2
    grad_query, grad_key, grad_value = [], [], []
    for part in range(2):
        rows = slice(part * step, (part + 1) * step)
        seen = (part + 1) * step
        shape = (seen, step)
        allowed = lax.broadcasted_iota(jnp.int32, shape, 1) + part * step >= (
            lax.broadcasted_iota(jnp.int32, shape, 0)
        )
        for head in range(2):
            mine = lanes[rows] // HEAD == head
            own = lanes[:seen] // HEAD == head
            q_one = jnp.where(mine, query[rows], jnp.zeros_like(query[rows]))
            g_one = jnp.where(mine, grad[rows], jnp.zeros_like(grad[rows]))
            k_one = jnp.where(own, key_scaled[:seen], jnp.zeros_like(key[:seen]))
            scores = jnp.where(allowed, dot_last(key[:seen], q_one), -1e30)
            top = jnp.max(scores, axis=0, keepdims=True)
            expo = jnp.exp(scores - top)
            total = jnp.sum(expo, axis=0, keepdims=True)
            probs = expo * (1.0 / total)
            grad_probs = dot_last(value[:seen], g_one)
            inner = jnp.sum(probs * grad_probs, axis=0, keepdims=True)
            grad_scores = (probs * (grad_probs - inner)).astype(jnp.bfloat16)
            rounded = probs.astype(jnp.bfloat16)
            grad_value.append(jnp.dot(rounded, g_one, preferred_element_type=jnp.float32))
            grad_key.append(jnp.dot(grad_scores, q_one, preferred_element_type=jnp.float32))
            grad_query.append(dot_first(grad_scores, k_one))

    def gather(parts):
        first = parts[0] + parts[1]
        second = parts[2] + parts[3]
        return jnp.concatenate([first + second[:step], second[step:]], axis=0)

    def unrotated(values):
        return (values * cosine - swap_halves(values, lanes) * sine).astype(jnp.bfloat16)

    all_query = jnp.concatenate(
        [grad_query[0] + grad_query[1], grad_query[2] + grad_query[3]], axis=0
    )
    columns = out_ref.shape[1] // 3
    place = pl.multiple_of(pl.program_id(0) * PAIR, PAIR)
    out_ref[:, pl.ds(place, PAIR)] = unrotated(all_query)
    out_ref[:, pl.ds(columns + place, PAIR)] = unrotated(gather(grad_key))
    out_ref[:, pl.ds(2 * columns + place, PAIR)] = gather(grad_value).astype(jnp.bfloat16)


def pair_block(offset):
    return pl.BlockSpec((LEN, PAIR), lambda step: (0, offset + step))


def whole_block(columns):
    return pl.BlockSpec((LEN, columns), lambda step: (0, 0))


def attention(qkv, cosine, sine):
    columns = qkv.shape[1] // 3
    pairs = columns // PAIR
    flat = jax.ShapeDtypeStruct((LEN, columns), jnp.bfloat16)
    return pl.pallas_call(
        forward_kernel,
        grid=(pairs,),
        in_specs=[pair_block(0), pair_block(pairs), pair_block(2 * pairs)]
        + [whole_block(PAIR)] * 2,
        out_specs=[pair_block(0)] * 4,
        out_shape=[flat] * 4,
        name="attend",
        cost_estimate=pl.CostEstimate(
            flops=8 * LEN * LEN * columns,
            transcendentals=LEN * LEN * columns // HEAD,
            bytes_accessed=20 * LEN * columns,
        ),
    )(qkv, qkv, qkv, cosine, sine)


def attention_back(query, key, value, grad, cosine, sine):
    columns = query.shape[1]
    return pl.pallas_call(
        backward_kernel,
        grid=(columns // PAIR,),
        in_specs=[pair_block(0)] * 4 + [whole_block(PAIR)] * 2,
        out_specs=whole_block(3 * columns),
        out_shape=jax.ShapeDtypeStruct((LEN, 3 * columns), jnp.bfloat16),
        name="attend_back",
        cost_estimate=pl.CostEstimate(
            flops=20 * LEN * LEN * columns,
            transcendentals=LEN * LEN * columns // HEAD,
            bytes_accessed=14 * LEN * columns,
        ),
    )(query, key, value, grad, cosine, sine)


TILE = 256


def unit_kernel(norm_ref, grad_ref, gate_ref, up_ref, down_ref, activ_ref, pre_ref):
    rows = norm_ref[...]
    gate = jnp.dot(rows, gate_ref[...], preferred_element_type=jnp.float32)
    up = jnp.dot(rows, up_ref[...], preferred_element_type=jnp.float32)
    grad_activ = jnp.dot(grad_ref[...], down_ref[...], preferred_element_type=jnp.float32)
    sigma = jax.nn.sigmoid(gate)
    swish = gate * sigma
    activ_ref[...] = (swish * up).astype(jnp.bfloat16)
    grad_gate = grad_activ * up * sigma * (1.0 + gate * (1.0 - sigma))
    place = pl.multiple_of(pl.program_id(0) * TILE, TILE)
    units = pre_ref.shape[1] // 2
    pre_ref[:, pl.ds(place, TILE)] = grad_gate.astype(jnp.bfloat16)
    pre_ref[:, pl.ds(units + place, TILE)] = (grad_activ * swish).astype(jnp.bfloat16)


def hidden_units_pass(normed, grads, gate_up, down):
    rows, width = normed.shape
    units = down.shape[1]
    steps = units // TILE
    whole = pl.BlockSpec((rows, width), lambda step: (0, 0))

    def tile(offset):
        return pl.BlockSpec((width, TILE), lambda step: (0, offset + step))

    return pl.pallas_call(
        unit_kernel,
        grid=(steps,),
        in_specs=[whole, whole, tile(0), tile(steps), tile(0)],
        out_specs=[
            pl.BlockSpec((rows, TILE), lambda step: (0, step)),
            pl.BlockSpec((rows, 2 * units), lambda step: (0, 0)),
        ],
        out_shape=[
            jax.ShapeDtypeStruct((rows, units), jnp.bfloat16),
            jax.ShapeDtypeStruct((rows, 2 * units), jnp.bfloat16),
        ],
        name="units",
        cost_estimate=pl.CostEstimate(
            flops=rows * width * units, transcendentals=0, bytes_accessed=4 * rows * width
        ),
    )(normed, grads, gate_up, gate_up, down)


def rows_kernel(left_ref, right_ref, out_ref):
    out_ref[...] = dot_last(left_ref[...], right_ref[...]).astype(out_ref.dtype)


def times_rows(left, right, dtype):
    rows, depth = left.shape
    width = right.shape[0]
    return pl.pallas_call(
        rows_kernel,
        grid=(width // TILE,),
        in_specs=[
            pl.BlockSpec((rows, depth), lambda step: (0, 0)),
            pl.BlockSpec((TILE, depth), lambda step: (step, 0)),
        ],
        out_specs=pl.BlockSpec((rows, TILE), lambda step: (0, step)),
        out_shape=jax.ShapeDtypeStruct((rows, width), dtype),
        name="sums",
        cost_estimate=pl.CostEstimate(
            flops=rows * width * depth // 4, transcendentals=0, bytes_accessed=rows * width
        ),
    )(left, right)


def shift(values, count):
    return lax.ppermute(values, "tensor", [(i, (i + 1) % count) for i in range(count)])


def after(values, *earlier):
    return lax.optimization_barrier((values,) + earlier)[0]


PEERS = 8
ORDER = (0, 2, 4, 6, 1, 3, 5, 7)


def peer(values, hop):
    return lax.ppermute(values, "dp", [(i, i ^ hop) for i in range(PEERS)])


def by_peer(values):
    width = values.shape[1] // PEERS
    blocks = [values[:, k * width : (k + 1) * width] for k in range(PEERS)]
    me = lax.axis_index("dp")
    for hop in (1, 2, 4):
        blocks = [jnp.where(me & hop, blocks[k ^ hop], blocks[k]) for k in range(PEERS)]
    half = PEERS // 2
    near = jnp.concatenate([blocks[k] for k in ORDER[:half]], axis=1)
    far = jnp.concatenate([blocks[k] for k in ORDER[half:]], axis=1)
    return near, far


def corner_step(kept, *stage):
    rows = kept.shape[0] // 4
    half = rows // 2
    mine, over_x, over_y, corner = [kept[k * rows : (k + 1) * rows] for k in range(4)]
    from_y = after(peer(corner[:half], 4), *stage)
    from_x = after(peer(corner[half:], 2), *stage)
    over_x = jnp.concatenate([over_x[:half] + from_y, over_x[half:]], axis=0)
    over_y = jnp.concatenate([over_y[:half], over_y[half:] + from_x], axis=0)
    return mine, over_x, over_y


def cross_step(mine, over_x, over_y):
    over_x, over_y = peer(over_x, 2), peer(over_y, 4)
    return mine.astype(jnp.float32) + over_x.astype(jnp.float32) + over_y.astype(jnp.float32)


def travel(values, count):
    stops = [values]
    for _ in range(count - 1):
        stops.append(shift(stops[-1], count))
    return stops


def ring_sum(parts, count):
    total = parts[1]
    for j in list(range(2, count)) + [0]:
        total = shift(total.astype(jnp.bfloat16), count).astype(jnp.float32) + parts[j]
    return total


def token_parallel(
    tokens, w_query, w_key, w_value, w_output, attn_gain, w_gate, w_up, w_down, mlp_gain, cotangent
):
    count = lax.axis_size("tensor")
    heads = w_query.shape[1]
    hidden_units = w_gate.shape[1]
    gains = lax.all_gather(jnp.stack([attn_gain, mlp_gain]), "dp", axis=0)
    gains = jnp.swapaxes(gains, 0, 1).reshape(2, -1).astype(jnp.float32)
    attn_scale, mlp_scale = gains[0], gains[1]
    shard = jnp.concatenate([w_query, w_key, w_value, w_output], axis=1)
    own = lax.all_gather(shard, "dp", axis=0, tiled=True)
    others = travel(shard, count)[1:]
    rest_shard = jnp.concatenate(
        [other[:, k * heads : (k + 1) * heads] for k in range(4) for other in others], axis=1
    )
    rest = lax.all_gather(rest_shard, "dp", axis=0, tiled=True)
    wide = (count - 1) * heads
    gate_up_shard = after(jnp.concatenate([w_gate, w_up], axis=1), rest_shard)
    gate_up = lax.all_gather(gate_up_shard, "dp", axis=0, tiled=True)
    down = lax.all_gather(after(w_down, rest_shard), "dp", axis=0, tiled=True)

    source = tokens.astype(jnp.float32)
    inverse_one = lax.rsqrt(jnp.mean(source * source, axis=-1, keepdims=True) + eps)
    normed_one = (source * inverse_one * attn_scale).astype(jnp.bfloat16)
    near_one, far_one = by_peer(normed_one)
    cosine, sine = lane_tables()
    own_qkv = jnp.dot(normed_one, own[:, : 3 * heads], preferred_element_type=jnp.float32)
    own_query, own_key, own_value, own_mixed = attention(own_qkv, cosine, sine)
    cotangents = [cotangent, shift(after(cotangent, others[-1]), count)]
    for _ in range(count - 2):
        cotangents.append(shift(after(cotangents[-1], own_mixed), count))
    rest = after(rest, *cotangents[:-1])
    rest_qkv = jnp.dot(normed_one, rest[:, : 3 * wide], preferred_element_type=jnp.float32)
    rest_query, rest_key, rest_value, rest_mixed = attention(rest_qkv, cosine, sine)
    branch = contract_cols(own_mixed, own[:, 3 * heads :])
    branch = branch + contract_cols(rest_mixed, rest[:, 3 * wide :])
    hidden = source + after(branch, cotangents[-1])
    inverse_two = lax.rsqrt(jnp.mean(hidden * hidden, axis=-1, keepdims=True) + eps)
    normed_two = (hidden * inverse_two * mlp_scale).astype(jnp.bfloat16)

    normed = travel(normed_two, count)
    activs, pres, norm_parts = [], [], []
    arrived = None
    for j in range(count):
        earlier = (normed[j + 1],) if j in (1, 2) else (norm_total,) if j == 3 else ()
        rows = after(normed[j], *earlier)
        activ, pre = hidden_units_pass(rows, cotangents[j], gate_up, down)
        norm_part = times_rows(pre, gate_up, jnp.float32)
        if j == 1:
            norm_total = norm_part.astype(jnp.bfloat16)
        elif j > 1:
            arrived = shift(norm_total, count)
            norm_total = (arrived.astype(jnp.float32) + norm_part).astype(jnp.bfloat16)
        activs.append(activ)
        pres.append(pre)
        norm_parts.append(norm_part)
    arrived = shift(norm_total, count)
    all_normed = jnp.concatenate(normed, axis=0)
    all_cotangents = jnp.concatenate(cotangents, axis=0)
    activs[-1] = after(activs[-1], norm_total)
    grad_down_w = contract_rows(all_cotangents, jnp.concatenate(activs, axis=0)).astype(
        jnp.bfloat16
    )
    pres[-1] = after(pres[-1], grad_down_w, norm_total)
    grad_gate_up_w = contract_rows(all_normed, jnp.concatenate(pres, axis=0)).astype(jnp.bfloat16)
    grad_normed_two = arrived.astype(jnp.float32) + after(
        norm_parts[0], grad_gate_up_w, grad_down_w
    )

    def over_dp(values):
        return lax.psum_scatter(values, "dp", scatter_dimension=0, tiled=True)

    grad_gate_up = over_dp(grad_gate_up_w).astype(jnp.float32)
    grad_down = over_dp(grad_down_w).astype(jnp.float32)

    grad_hidden_norm, mlp_gain_part = norm_back(grad_normed_two, hidden, inverse_two, mlp_scale)
    grad_hidden = cotangent.astype(jnp.float32) + grad_hidden_norm
    grad_branch = grad_hidden.astype(jnp.bfloat16)
    all_mixed = jnp.concatenate([own_mixed, rest_mixed], axis=1)
    near_branch, far_branch = by_peer(grad_branch)
    output_far = contract_rows(far_branch, all_mixed).astype(jnp.bfloat16)
    rest_grad = jnp.dot(
        after(grad_branch, output_far), rest[:, 3 * wide :], preferred_element_type=jnp.float32
    ).astype(jnp.bfloat16)
    output_near = contract_rows(near_branch, after(all_mixed, rest_grad))
    output_near = (output_near + peer(output_far, 1).astype(jnp.float32)).astype(jnp.bfloat16)
    rest_grad = after(rest_grad, output_near, grad_down)
    rest_pre = attention_back(rest_query, rest_key, rest_value, rest_grad, cosine, sine)
    output_parts = corner_step(output_near, rest_pre)

    def mlp_part(j, stage):
        return times_rows(after(activs[j], stage), down, jnp.bfloat16)

    mlp_arrived = shift(mlp_part(1, grad_branch), count)
    mlp_next = mlp_part(2, output_far)
    rest_pre = after(rest_pre, mlp_arrived, *output_parts)
    mlp_total = (mlp_arrived.astype(jnp.float32) + after(mlp_next, rest_pre)).astype(jnp.bfloat16)
    mlp_arrived = shift(mlp_total, count)
    rest_far = contract_rows(far_one, rest_pre).astype(jnp.bfloat16)
    output_sum = cross_step(*output_parts)
    rest_later = after(rest_pre, rest_far)
    grad_normed_one = contract_cols(rest_later, rest[:, : 3 * wide])
    rest_later = after(rest_later, grad_normed_one)
    rest_near = contract_rows(near_one, rest_later) + peer(rest_far, 1).astype(jnp.float32)
    rest_near = rest_near.astype(jnp.bfloat16)
    rest_parts = corner_step(rest_near)
    own_grad = jnp.dot(
        after(grad_branch, rest_near), own[:, 3 * heads :], preferred_element_type=jnp.float32
    ).astype(jnp.bfloat16)
    own_pre = attention_back(own_query, own_key, own_value, own_grad, cosine, sine)
    own_pre = after(own_pre, mlp_arrived, grad_gate_up, output_sum, *rest_parts)
    mlp_next = after(mlp_part(3, rest_far), own_pre)
    mlp_total = (mlp_arrived.astype(jnp.float32) + mlp_next).astype(jnp.bfloat16)
    mlp_total = shift(mlp_total, count).astype(jnp.float32) + mlp_part(0, rest_near)
    rest_sum = cross_step(*rest_parts)
    own_far = contract_rows(far_one, own_pre).astype(jnp.bfloat16)
    own_later = after(own_pre, own_far)
    grad_normed_one = grad_normed_one + contract_cols(own_later, own[:, : 3 * heads])
    own_near = contract_rows(near_one, own_later) + peer(own_far, 1).astype(jnp.float32)
    own_sum = cross_step(*corner_step(own_near.astype(jnp.bfloat16)))
    block_out = (hidden + mlp_total).astype(jnp.bfloat16)

    grad_source_norm, attn_gain_part = norm_back(grad_normed_one, source, inverse_one, attn_scale)
    grad_tokens = (grad_hidden + grad_source_norm).astype(jnp.bfloat16)

    def group_slot(j):
        if not j:
            return own_sum
        columns = [rest_sum[:, k * wide + (j - 1) * heads : k * wide + j * heads] for k in range(3)]
        return jnp.concatenate(columns, axis=1)

    qkv = ring_sum([group_slot(j) for j in range(count)], count)
    grad_query, grad_key, grad_value = [qkv[:, k * heads : (k + 1) * heads] for k in range(3)]
    grad_output = ring_sum(
        [output_sum[:, j * heads : (j + 1) * heads].astype(jnp.float32) for j in range(count)], count
    )
    gain_sums = lax.psum_scatter(
        jnp.stack([attn_gain_part, mlp_gain_part]),
        ("dp", "tensor"),
        scatter_dimension=1,
        tiled=True,
    )
    return (
        block_out,
        grad_tokens,
        grad_query,
        grad_key,
        grad_value,
        grad_output,
        gain_sums[0],
        grad_gate_up[:, :hidden_units],
        grad_gate_up[:, hidden_units:],
        grad_down,
        gain_sums[1],
    )


def local(tokens, w_query, *others):
    axes = (lax.axis_size("dp"), lax.axis_size("tensor"))
    whole = tokens.shape[0] == LEN and w_query.shape[1] % PAIR == 0
    if whole and axes[0] == PEERS and axes[1] == 4:
        return token_parallel(tokens, w_query, *others)
    return tensor_parallel(tokens, w_query, *others)


def solution(mesh):
    in_specs = (
        P(("dp", "tensor"), None),
        P("dp", "tensor"),
        P("dp", "tensor"),
        P("dp", "tensor"),
        P("dp", "tensor"),
        P("dp"),
        P("dp", "tensor"),
        P("dp", "tensor"),
        P("dp", "tensor"),
        P("dp"),
        P(("dp", "tensor"), None),
    )
    out_specs = (
        P(("dp", "tensor"), None),
        P(("dp", "tensor"), None),
        P("dp", "tensor"),
        P("dp", "tensor"),
        P("dp", "tensor"),
        P("dp", "tensor"),
        P(("dp", "tensor")),
        P("dp", "tensor"),
        P("dp", "tensor"),
        P("dp", "tensor"),
        P(("dp", "tensor")),
    )
    return jax.shard_map(local, mesh=mesh, in_specs=in_specs, out_specs=out_specs, check_vma=False)
```
